256 devices in a mesh: dp: 8 (over z), pipe: 4 (over y), expert: 8 (over x, core).
Axes of the slice: x: 4, y: 4, z: 8, core: 2. Of those that a mesh axis runs over, the one named last changes fastest.
Arguments:
- fresh: bfloat16 [4096, 6144], P(('dp', 'expert')), may hold values from -6 to 6
- cotangent: bfloat16 [4096, 6144], P(('dp', 'expert')), may hold values from -6 to 6
- prev_out: bfloat16 [4, 4096, 6144], P('pipe', ('dp', 'expert')), may hold values from -6 to 6
- prev_grad: bfloat16 [4, 4096, 6144], P('pipe', ('dp', 'expert')), may hold values from -6 to 6
- saved_in: bfloat16 [4, 4096, 6144], P('pipe', ('dp', 'expert')), may hold values from -6 to 6
- route_fwd: int32 [4, 4096, 2], P('pipe', ('dp', 'expert')), may hold values from 0 to 7, all different within a row; in each aligned block of 64 rows (0 to 63, 64 to 127, ..., all dimensions but the last counted through in order) at most 32 rows name the same one
- route_bwd: int32 [4, 4096, 2], P('pipe', ('dp', 'expert')), may hold values from 0 to 7, all different within a row; in each aligned block of 64 rows (0 to 63, 64 to 127, ..., all dimensions but the last counted through in order) at most 32 rows name the same one
- router: bfloat16 [4, 6144, 8], P('pipe'), may hold values from -0.078125 to 0.078125
- gate_up: bfloat16 [4, 8, 6144, 256], P('pipe', 'expert'), may hold values from -0.078125 to 0.078125
- down: bfloat16 [4, 8, 128, 6144], P('pipe', 'expert'), may hold values from -0.5 to 0.5
Outputs:
- section_out: bfloat16 [4, 4096, 6144], P('pipe', ('dp', 'expert'))
- input_grad: bfloat16 [4, 4096, 6144], P('pipe', ('dp', 'expert'))
- grad_gate_up: bfloat16 [4, 8, 6144, 256], P('pipe', 'expert', 'dp')
- grad_down: bfloat16 [4, 8, 128, 6144], P('pipe', 'expert', None, 'dp')
- grad_router: float32 [4, 6144, 8], P('pipe', ('dp', 'expert'))
The draws below stay inside these ranges and needn't reach their ends.
Inputs may be any that keep to these rules, and one draw needn't show every extreme that they name: `route_fwd`: each row names two different experts; in the 64 rows of one device no expert is named by more than 32 rows, and some expert reaches 32. `route_bwd`: each row names two different experts; in the 64 rows of one device no expert is named by more than 32 rows, and some expert reaches 32.
All inputs are finite; a program needn't handle non-finite values.
Results may differ from the reference program's by a relative error of at most 0.015.
Values may be sent and summed in bfloat16 or wider, within the bound.
No kernel may reach another device: no remote copies, remote signals or barrier semaphores. Data moves between devices by JAX's collectives and lax.ppermute only.
A program may use at most 128 MiB of HBM per device.

```python
import math
import jax
import jax.numpy as jnp
import numpy as np
from jax import lax

D = 6144
FF = 128
TOK = 64
SECTIONS = 4
EXPERTS = 8
TOKENS = 4096
CAP = 32
CAP2 = 4
N_DP = 8
N_EXPERT = 8


def levels(own_key, dims, pieces, smallest, top_value):
    loudness = 1.0
    for axis_at, blocks in pieces:
        heights = jax.random.uniform(jax.random.fold_in(jax.random.fold_in(own_key, 6), axis_at), (blocks,), jnp.float32, smallest / len(pieces), top_value / len(pieces))
        loudness = loudness * jnp.repeat(jnp.exp(heights), dims[axis_at] // blocks).reshape((-1,) + (1,) * (len(dims) - 1 - axis_at))
    return loudness


def deal_out(stream_key, own, number, rows, count, top, reach, lean):
    sequence = jax.random.permutation(stream_key, count)
    crowded, usual = load_shares(count, rows * top, reach, lean, True), load_shares(count, rows * top, reach, lean, False)
    places = jnp.arange(count)

    def named(tallies, offset_by):
        used = int((tallies > 0).sum())
        fixed = max(1, used // 4)
        passed = fixed + (places - fixed + offset_by * (used - fixed)) % max(1, count - fixed)
        return jnp.zeros((count,), jnp.int32).at[sequence[jnp.where(places < fixed, places, passed)]].set(jnp.asarray(tallies, jnp.int32))

    tallies = jnp.where(number % 4 == 0, named(crowded, number // 4), named(usual, number - number // 4 - 1))
    mixed = jax.random.permutation(jax.random.fold_in(own, 3), count)
    donor, taker = mixed[0:count // 2 * 2:2], mixed[1:count // 2 * 2:2]
    slack = jnp.minimum(tallies[donor] - 1, reach - tallies[taker]) // 2
    slack = jnp.where((donor == sequence[0]) | (taker == sequence[0]) | (tallies[taker] == 0), 0, jnp.maximum(slack, 0))
    passed = jax.random.randint(jax.random.fold_in(own, 4), (count // 2,), 0, 1 << 20) % (slack + 1)
    tallies = tallies.at[donor].add(-passed).at[taker].add(passed)
    members = jnp.searchsorted(jnp.cumsum(tallies), jnp.arange(rows * top), side="right").astype(jnp.int32)
    listing = members.reshape(top, rows).T
    listing = listing[jax.random.permutation(jax.random.fold_in(own, 1), rows)]
    offset_by = jax.random.randint(jax.random.fold_in(own, 2), (rows, 1), 0, top)
    return jnp.take_along_axis(listing, (jnp.arange(top)[None, :] + offset_by) % top, axis=1)


def load_shares(amount, total, most, slope, full):
    loads = [(1 << 20) // math.isqrt(standing ** slope) + 1 for standing in range(1, amount + 1)]
    largest = most if full else min(most, max(-(-total // amount), total * loads[0] // sum(loads)))
    least = 1 if total - largest >= amount - 1 else 0
    counts, surplus = [largest] + [least] * (amount - 1), total - largest - least * (amount - 1)
    while surplus > 0:
        candidates = [i for i in range(1, amount) if counts[i] < largest] or [i for i in range(1, amount) if counts[i] < most]
        whole, budget = sum([loads[i] for i in candidates]), surplus
        for i in candidates:
            more = min(most - counts[i], max(1, budget * loads[i] // whole), surplus)
            counts[i] = counts[i] + more
            surplus = surplus - more
    return np.array(counts)


def noise(own_key, dims, scale, bound, pieces=(), kind=jnp.bfloat16):
    factor_of = levels(own_key, dims, pieces, -0.22, 0.18) if pieces else 1.0
    drawn = jax.random.normal(own_key, dims, jnp.float32) * scale * factor_of
    return jnp.minimum(jnp.maximum(drawn, -bound), bound).astype(kind)


def setup_inputs(seed: int = 0) -> dict:
    keys = jax.random.split(jax.random.key(seed), 11)
    fresh = noise(keys[0], (TOKENS, D), 1.0, 6.0, ((0, 64),))
    cotangent = noise(keys[1], (TOKENS, D), 1.0, 6.0, ((0, 64),))
    prev_out = noise(keys[2], (SECTIONS, TOKENS, D), 1.0, 6.0, ((0, 4), (1, 64)))
    prev_grad = noise(keys[3], (SECTIONS, TOKENS, D), 1.0, 6.0, ((0, 4), (1, 64)))
    saved_in = noise(keys[4], (SECTIONS, TOKENS, D), 1.0, 6.0, ((0, 4), (1, 64)))
    route_fwd_keys = jax.random.split(jax.random.fold_in(keys[5], 1), SECTIONS * TOKENS // TOK)
    route_fwd_turns = jax.random.permutation(jax.random.fold_in(keys[5], 3), SECTIONS * TOKENS // TOK)
    route_fwd = jax.vmap(lambda own, number: deal_out(jax.random.fold_in(keys[5], 2), own, number, TOK, EXPERTS, 2, CAP, 2))(route_fwd_keys, route_fwd_turns).reshape((SECTIONS, TOKENS, 2))
    route_bwd_keys = jax.random.split(jax.random.fold_in(keys[6], 1), SECTIONS * TOKENS // TOK)
    route_bwd_turns = jax.random.permutation(jax.random.fold_in(keys[6], 3), SECTIONS * TOKENS // TOK)
    route_bwd = jax.vmap(lambda own, number: deal_out(jax.random.fold_in(keys[6], 2), own, number, TOK, EXPERTS, 2, CAP, 2))(route_bwd_keys, route_bwd_turns).reshape((SECTIONS, TOKENS, 2))
    router = noise(keys[7], (SECTIONS, D, EXPERTS), D ** -0.5, 0.078125, ((0, 4),))
    gate_up = noise(keys[8], (SECTIONS, EXPERTS, D, 2 * FF), D ** -0.5, 0.078125, ((0, 4), (1, 8)))
    down = noise(keys[9], (SECTIONS, EXPERTS, FF, D), FF ** -0.5, 0.5, ((0, 4), (1, 8)))
    return dict(fresh=fresh, cotangent=cotangent, prev_out=prev_out, prev_grad=prev_grad, saved_in=saved_in, route_fwd=route_fwd, route_bwd=route_bwd, router=router, gate_up=gate_up, down=down)


EPSILON = 1e-05

def normalize(values_in):
    values = values_in.astype(jnp.float32)
    spread = jnp.sqrt(lax.optimization_barrier(jnp.mean(values * values, axis=-1, keepdims=True)) + EPSILON)
    return (values / spread, spread)

def gate_pair(normed, router_w, routes):
    logits = jnp.dot(normed, router_w, preferred_element_type=jnp.float32)
    onehot = (routes[:, :, None] == jnp.arange(EXPERTS, dtype=jnp.int32)[None, None, :]).astype(jnp.float32)
    chosen = lax.optimization_barrier(jnp.sum(onehot * logits[:, None, :], axis=2))
    first_gate = jax.nn.sigmoid(chosen[:, 0] - chosen[:, 1])
    second_gate = jax.nn.sigmoid(chosen[:, 1] - chosen[:, 0])
    return (first_gate, second_gate, onehot)

def expert_forward(inputs, gate_up_w, down_w):
    projected = jnp.dot(inputs, gate_up_w, preferred_element_type=jnp.float32)
    pre_gate = projected[:, :FF]
    pre_up = projected[:, FF:]
    hidden = (pre_gate * jax.nn.sigmoid(pre_gate) * pre_up).astype(jnp.bfloat16)
    return jnp.dot(hidden, down_w, preferred_element_type=jnp.float32).astype(jnp.bfloat16)

def expert_backward(inputs, upstream, weight, gate_up_w, down_w):
    projected = jnp.dot(inputs, gate_up_w, preferred_element_type=jnp.float32)
    pre_gate = projected[:, :FF]
    pre_up = projected[:, FF:]
    sigmoid_gate = jax.nn.sigmoid(pre_gate)
    active = pre_gate * sigmoid_gate
    hidden = (active * pre_up).astype(jnp.bfloat16)
    output = jnp.dot(hidden, down_w, preferred_element_type=jnp.float32).astype(jnp.bfloat16)
    gate_grad = lax.optimization_barrier(jnp.sum(upstream.astype(jnp.float32) * output.astype(jnp.float32), axis=1)).astype(jnp.bfloat16)
    out_grad = (weight.astype(jnp.float32)[:, None] * upstream.astype(jnp.float32)).astype(jnp.bfloat16)
    hidden_grad = jnp.dot(out_grad, down_w.T, preferred_element_type=jnp.float32)
    grad_g = hidden_grad * pre_up * sigmoid_gate * (1.0 + pre_gate * (1.0 - sigmoid_gate))
    grad_u = hidden_grad * active
    pre_grad = jnp.concatenate([grad_g, grad_u], axis=1).astype(jnp.bfloat16)
    row_grad = jnp.dot(pre_grad, gate_up_w.T, preferred_element_type=jnp.float32).astype(jnp.bfloat16)
    gate_up_part = jnp.dot(inputs.T, pre_grad, preferred_element_type=jnp.float32).astype(jnp.bfloat16)
    down_part = jnp.dot(hidden.T, out_grad, preferred_element_type=jnp.float32).astype(jnp.bfloat16)
    return (row_grad, gate_grad, gate_up_part, down_part)

def route_rows(routes_all):
    device_count = N_DP * N_EXPERT
    blocks = routes_all.reshape(device_count, TOK * 2)
    sources = jnp.arange(device_count, dtype=jnp.int32)
    onehot = (blocks[:, :, None] == jnp.arange(EXPERTS, dtype=jnp.int32)[None, None, :]).astype(jnp.int32)
    position = lax.optimization_barrier(jnp.sum((jnp.cumsum(onehot, axis=1) - onehot) * onehot, axis=2))
    replica = ((sources // N_EXPERT)[:, None] + position) % N_DP
    target = replica * N_EXPERT + blocks
    landing = sources[:, None] * CAP2 + position // N_DP
    return (target.reshape(-1).astype(jnp.int32), landing.reshape(-1).astype(jnp.int32))

def moe_forward(packed, routes_all, gate_up_s, down_s):
    target, landing = route_rows(routes_all)
    copies = jnp.repeat(packed, 2, axis=0)
    buffer_rows = N_DP * N_EXPERT * CAP2

    def visit(holding, device):
        matches = target == device
        landing_row = jnp.where(matches, landing, buffer_rows)
        buffer = jnp.zeros((buffer_rows, D), jnp.bfloat16).at[landing_row].set(copies, mode='drop')
        owner_index = device % N_EXPERT
        result = expert_forward(buffer, gate_up_s[owner_index], down_s[owner_index])
        picked = result[jnp.minimum(landing_row, buffer_rows - 1)]
        return (jnp.where(matches[:, None], picked, holding), None)
    final_state, ignored = lax.scan(visit, jnp.zeros_like(copies), jnp.arange(N_DP * N_EXPERT, dtype=jnp.int32))
    return final_state.reshape(TOKENS, 2, D)

def moe_backward(packed, upstream, weights_flat, routes_all, gate_up_s, down_s):
    target, landing = route_rows(routes_all)
    copies = jnp.repeat(packed, 2, axis=0)
    upstream_copies = jnp.repeat(upstream, 2, axis=0)
    buffer_rows = N_DP * N_EXPERT * CAP2

    def visit(holding, device):
        rows_state, gate_state, gate_up_acc, down_acc = holding
        matches = target == device
        landing_row = jnp.where(matches, landing, buffer_rows)
        buffer = jnp.zeros((buffer_rows, D), jnp.bfloat16).at[landing_row].set(copies, mode='drop')
        buffer_up = jnp.zeros((buffer_rows, D), jnp.bfloat16).at[landing_row].set(upstream_copies, mode='drop')
        buffer_weight = jnp.zeros((buffer_rows,), jnp.bfloat16).at[landing_row].set(weights_flat, mode='drop')
        owner_index = device % N_EXPERT
        row_grad, gate_grad, gate_up_part, down_part = expert_backward(buffer, buffer_up, buffer_weight, gate_up_s[owner_index], down_s[owner_index])
        clipped = jnp.minimum(landing_row, buffer_rows - 1)
        rows_state = jnp.where(matches[:, None], row_grad[clipped], rows_state)
        gate_state = jnp.where(matches, gate_grad[clipped], gate_state)
        gate_up_acc = gate_up_acc.at[owner_index].add(gate_up_part.astype(jnp.float32))
        down_acc = down_acc.at[owner_index].add(down_part.astype(jnp.float32))
        return ((rows_state, gate_state, gate_up_acc, down_acc), None)
    start = (jnp.zeros_like(copies), jnp.zeros((2 * TOKENS,), jnp.bfloat16), jnp.zeros((EXPERTS, D, 2 * FF), jnp.float32), jnp.zeros((EXPERTS, FF, D), jnp.float32))
    final_state, ignored = lax.scan(visit, start, jnp.arange(N_DP * N_EXPERT, dtype=jnp.int32))
    rows_state, gate_state, gate_up_acc, down_acc = final_state
    return (rows_state.reshape(TOKENS, 2, D), gate_state.reshape(TOKENS, 2), gate_up_acc, down_acc)

def reference(fresh, cotangent, prev_out, prev_grad, saved_in, route_fwd, route_bwd, router, gate_up, down):
    outputs_fwd = []
    outputs_bwd = []
    grads_gate_up = []
    grads_down = []
    grads_router = []
    for section_index in range(SECTIONS):
        inputs_fwd = fresh if section_index == 0 else prev_out[section_index - 1]
        upstream = cotangent if section_index == SECTIONS - 1 else prev_grad[section_index + 1]
        inputs_bwd = saved_in[section_index]
        router_w = router[section_index]
        unit_fwd, spread_fwd = normalize(inputs_fwd)
        packed_fwd = unit_fwd.astype(jnp.bfloat16)
        first_fwd, second_fwd, onehot_fwd = gate_pair(packed_fwd, router_w, route_fwd[section_index])
        chosen = moe_forward(packed_fwd, route_fwd[section_index], gate_up[section_index], down[section_index])
        section_value = inputs_fwd.astype(jnp.float32) + first_fwd[:, None] * chosen[:, 0].astype(jnp.float32) + second_fwd[:, None] * chosen[:, 1].astype(jnp.float32)
        outputs_fwd.append(section_value.astype(jnp.bfloat16))
        unit_bwd, spread_bwd = normalize(inputs_bwd)
        packed_bwd = unit_bwd.astype(jnp.bfloat16)
        first_bwd, second_bwd, onehot_bwd = gate_pair(packed_bwd, router_w, route_bwd[section_index])
        weights_flat = jnp.stack([first_bwd, second_bwd], axis=1).reshape(-1).astype(jnp.bfloat16)
        row_grads, gate_grads, gate_up_acc, down_acc = moe_backward(packed_bwd, upstream, weights_flat, route_bwd[section_index], gate_up[section_index], down[section_index])
        gate_float = gate_grads.astype(jnp.float32)
        logit_step = first_bwd * second_bwd * (gate_float[:, 0] - gate_float[:, 1])
        logit_grad = (onehot_bwd[:, 0, :] - onehot_bwd[:, 1, :]) * logit_step[:, None]
        normed_grad = row_grads[:, 0].astype(jnp.float32) + row_grads[:, 1].astype(jnp.float32)
        normed_grad = normed_grad + jnp.dot(logit_grad, router_w.astype(jnp.float32).T, precision=lax.Precision.HIGHEST)
        router_grad = jnp.dot(packed_bwd.astype(jnp.float32).T, logit_grad, precision=lax.Precision.HIGHEST)
        inner_mean = lax.optimization_barrier(jnp.mean(normed_grad * unit_bwd, axis=1, keepdims=True))
        grad_value = upstream.astype(jnp.float32) + (normed_grad - unit_bwd * inner_mean) / spread_bwd
        outputs_bwd.append(grad_value.astype(jnp.bfloat16))
        grads_gate_up.append(gate_up_acc.astype(jnp.bfloat16))
        grads_down.append(down_acc.astype(jnp.bfloat16))
        grads_router.append(router_grad)
    return (jnp.stack(outputs_fwd), jnp.stack(outputs_bwd), jnp.stack(grads_gate_up), jnp.stack(grads_down), jnp.stack(grads_router))
```

```python
import jax
import jax.numpy as jnp
from jax import lax
from jax.sharding import PartitionSpec as P

EPSILON = 1e-05
LANES = 128


def passed_along(x, axis, by):
    length = lax.axis_size(axis)
    pairs = [(i, i + by) for i in range(length) if 0 <= i + by < length]
    return lax.ppermute(x, axis, pairs)


def ring_pairs(away):
    chips = lax.axis_size("expert") // 2
    pairs = []
    for chip in range(chips):
        for core in range(2):
            step = away if core == 0 else -away
            pairs.append((2 * chip + core, 2 * ((chip + step) % chips) + core))
    return pairs


def ahead(x):
    return lax.ppermute(x, "expert", ring_pairs(1))


def behind(x):
    return lax.ppermute(x, "expert", ring_pairs(-1))


def swapped(x):
    return lax.ppermute(x, "expert", [(i, i ^ 1) for i in range(lax.axis_size("expert"))])


def gather(block):
    near = ahead(block)
    back = behind(block)
    own_other = swapped(block)
    far = ahead(near)
    near_other = swapped(near)
    back_other = swapped(back)
    far_other = swapped(far)
    return [block, own_other, near, near_other, back, back_other, far, far_other]


def scatter_sum(blocks):
    own, own_other, near, near_other, back, back_other, far, far_other = blocks

    def both(mine, other):
        return (mine.astype(jnp.float32) + swapped(other).astype(jnp.float32)).astype(jnp.bfloat16)

    far = both(far, far_other)
    passing = behind(far)
    back = both(back, back_other)
    from_back = ahead(back)
    near = near.astype(jnp.float32) + swapped(near_other).astype(jnp.float32)
    near = (near + passing.astype(jnp.float32)).astype(jnp.bfloat16)
    from_near = behind(near)
    return (
        own.astype(jnp.float32)
        + swapped(own_other).astype(jnp.float32)
        + from_back.astype(jnp.float32)
        + from_near.astype(jnp.float32)
    )


def contract_rows(first_operand, second_operand):
    return lax.dot_general(
        first_operand, second_operand, (((0,), (0,)), ((), ())), preferred_element_type=jnp.float32
    )


def contract_cols(first_operand, second_operand):
    return lax.dot_general(
        first_operand, second_operand, (((1,), (1,)), ((), ())), preferred_element_type=jnp.float32
    )


def inverse_spread(values):
    values = values.astype(jnp.float32)
    return lax.rsqrt(jnp.mean(values * values, axis=-1, keepdims=True) + EPSILON)


def gate_table(normed, router_w, routes):
    experts = router_w.shape[1]
    logits = jnp.dot(normed, router_w, preferred_element_type=jnp.float32)
    onehot = (routes[:, :, None] == jnp.arange(experts, dtype=jnp.int32)[None, None, :]).astype(
        jnp.float32
    )
    chosen = jnp.sum(onehot * logits[:, None, :], axis=2)
    first_gate = jax.nn.sigmoid(chosen[:, 0] - chosen[:, 1])
    second_gate = jax.nn.sigmoid(chosen[:, 1] - chosen[:, 0])
    table = onehot[:, 0, :] * first_gate[:, None] + onehot[:, 1, :] * second_gate[:, None]
    return (first_gate, second_gate, onehot, table)


def halves(values):
    high = lax.reduce_precision(values, exponent_bits=8, mantissa_bits=7)
    return (high.astype(jnp.bfloat16), (values - high).astype(jnp.bfloat16))


def side_columns(table, inverse):
    table_high, table_low = halves(table)
    inverse_high, inverse_low = halves(inverse)
    columns = jnp.concatenate([table_high, table_low, inverse_high, inverse_low], axis=1)
    return jnp.pad(columns, ((0, 0), (0, LANES - columns.shape[1])))


def read_side(columns, experts, mine):
    columns = columns.astype(jnp.float32)
    hot = (jnp.arange(experts, dtype=jnp.int32) == mine).astype(jnp.float32)[None, :]
    table = columns[:, :experts] + columns[:, experts : 2 * experts]
    weight = jnp.sum(table * hot, axis=1, keepdims=True)
    inverse = columns[:, 2 * experts : 2 * experts + 1] + columns[:, 2 * experts + 1 : 2 * experts + 2]
    return (weight, inverse)


def shards(
    fresh, cotangent, prev_out, prev_grad, saved_in, route_fwd, route_bwd, router, gate_up, down
):
    section_index = lax.axis_index("pipe")
    sections = lax.axis_size("pipe")
    replicas = lax.axis_size("dp")
    owners = lax.axis_size("expert")
    mine = lax.axis_index("expert")
    inputs_bwd = saved_in[0]
    router_w = router[0]
    gate_up_w = gate_up[0, 0]
    down_w = down[0, 0]
    tokens, width = fresh.shape
    experts = router_w.shape[1]
    hidden_width = down_w.shape[0]

    returned = passed_along(prev_grad[0], "pipe", -1)
    arrived = passed_along(prev_out[0], "pipe", 1)
    rows_bwd = gather(inputs_bwd)
    inverse_bwd = inverse_spread(inputs_bwd)
    unit_bwd = inputs_bwd.astype(jnp.float32) * inverse_bwd
    first_bwd, second_bwd, onehot_bwd, table_bwd = gate_table(
        unit_bwd.astype(jnp.bfloat16), router_w, route_bwd[0]
    )
    upstream = jnp.where(section_index == sections - 1, cotangent, returned)
    ups = gather(jnp.concatenate([upstream, side_columns(table_bwd, inverse_bwd)], axis=1))

    inputs_fwd = jnp.where(section_index == 0, fresh, arrived)
    inverse_fwd = inverse_spread(inputs_fwd)
    normed_fwd = (inputs_fwd.astype(jnp.float32) * inverse_fwd).astype(jnp.bfloat16)
    table_fwd = gate_table(normed_fwd, router_w, route_fwd[0])[3]
    rows_fwd = gather(jnp.concatenate([inputs_fwd, side_columns(table_fwd, inverse_fwd)], axis=1))

    rows = jnp.concatenate(rows_bwd, axis=0)
    ups = jnp.concatenate(ups, axis=0)
    weight, inverse = read_side(ups[:, width:], experts, mine)
    ups = ups[:, :width]
    projected = jnp.dot(rows, gate_up_w, preferred_element_type=jnp.float32) * inverse
    pre_gate = projected[:, :hidden_width]
    pre_up = projected[:, hidden_width:]
    sigmoid_gate = jax.nn.sigmoid(pre_gate)
    active = pre_gate * sigmoid_gate
    hidden = active * pre_up
    bare_grad = contract_cols(ups, down_w)
    gate_grad = jnp.sum(hidden * bare_grad, axis=1, keepdims=True)
    hidden_grad = bare_grad * weight
    grad_g = hidden_grad * pre_up * sigmoid_gate * (1.0 + pre_gate * (1.0 - sigmoid_gate))
    grad_u = hidden_grad * active
    pre_grad = jnp.concatenate([grad_g, grad_u], axis=1)
    gate_up_part = contract_rows(rows, (pre_grad * inverse).astype(jnp.bfloat16))
    down_part = contract_rows((hidden * weight).astype(jnp.bfloat16), ups)
    grad_gate_up = lax.psum_scatter(
        gate_up_part.astype(jnp.bfloat16), "dp", scatter_dimension=0, tiled=True
    )
    grad_down = lax.psum_scatter(
        down_part.astype(jnp.bfloat16), "dp", scatter_dimension=1, tiled=True
    )
    row_grad = contract_cols(pre_grad.astype(jnp.bfloat16), gate_up_w).astype(jnp.bfloat16)
    gate_side = gate_grad * (jnp.arange(LANES, dtype=jnp.int32) == mine).astype(jnp.float32)[None, :]
    row_grad = jnp.concatenate([row_grad, gate_side.astype(jnp.bfloat16)], axis=1)
    back_rows = scatter_sum(
        [row_grad[i * tokens : (i + 1) * tokens] for i in range(owners)]
    )

    rows = jnp.concatenate(rows_fwd, axis=0)
    weight, inverse = read_side(rows[:, width:], experts, mine)
    projected = jnp.dot(rows[:, :width], gate_up_w, preferred_element_type=jnp.float32) * inverse
    pre_gate = projected[:, :hidden_width]
    pre_up = projected[:, hidden_width:]
    hidden = pre_gate * jax.nn.sigmoid(pre_gate) * pre_up * weight
    results = jnp.dot(
        hidden.astype(jnp.bfloat16), down_w, preferred_element_type=jnp.float32
    ).astype(jnp.bfloat16)

    gates_back = back_rows[:, width : width + experts]
    gate_first = jnp.sum(onehot_bwd[:, 0, :] * gates_back, axis=1)
    gate_second = jnp.sum(onehot_bwd[:, 1, :] * gates_back, axis=1)
    logit_step = first_bwd * second_bwd * (gate_first - gate_second)
    logit_grad = (onehot_bwd[:, 0, :] - onehot_bwd[:, 1, :]) * logit_step[:, None]
    router_part = lax.dot_general(
        logit_grad,
        unit_bwd.astype(jnp.bfloat16).astype(jnp.float32),
        (((0,), (0,)), ((), ())),
        precision=lax.Precision.HIGHEST,
        preferred_element_type=jnp.float32,
    )
    share = width // (replicas * owners)
    router_part = router_part.reshape(experts, replicas * owners, share).transpose(1, 0, 2)
    router_part = router_part.reshape(replicas * owners, experts * share)
    grad_router = lax.psum_scatter(router_part, ("dp", "expert"), scatter_dimension=0, tiled=True)
    grad_router = grad_router.reshape(experts, share).T
    normed_grad = back_rows[:, :width] + jnp.dot(
        logit_grad, router_w.astype(jnp.float32).T, precision=lax.Precision.HIGHEST
    )
    inner_mean = jnp.mean(normed_grad * unit_bwd, axis=1, keepdims=True)
    grad_value = upstream.astype(jnp.float32) + (normed_grad - unit_bwd * inner_mean) * inverse_bwd
    input_grad = grad_value.astype(jnp.bfloat16)

    back_fwd = scatter_sum([results[i * tokens : (i + 1) * tokens] for i in range(owners)])
    section_out = (inputs_fwd.astype(jnp.float32) + back_fwd).astype(jnp.bfloat16)
    return (
        section_out[None],
        input_grad[None],
        grad_gate_up[None, None],
        grad_down[None, None],
        grad_router[None],
    )


def solution(mesh):
    placed = (
        P(("dp", "expert"), None),
        P(("dp", "expert"), None),
        P("pipe", ("dp", "expert"), None),
        P("pipe", ("dp", "expert"), None),
        P("pipe", ("dp", "expert"), None),
        P("pipe", ("dp", "expert"), None),
        P("pipe", ("dp", "expert"), None),
        P("pipe", None, None),
        P("pipe", "expert", None, None),
        P("pipe", "expert", None, None),
    )
    return jax.shard_map(
        shards,
        mesh=mesh,
        in_specs=placed,
        out_specs=(
            P("pipe", ("dp", "expert"), None),
            P("pipe", ("dp", "expert"), None),
            P("pipe", "expert", "dp", None),
            P("pipe", "expert", None, "dp"),
            P("pipe", ("dp", "expert"), None),
        ),
        check_vma=False,
    )
```

```python
import functools

import jax
import jax.numpy as jnp
from jax import lax
from jax.experimental import pallas as pl
from jax.experimental.pallas import tpu as pltpu
from jax.sharding import PartitionSpec as P

EPSILON = 1e-05
LANES = 128
ROUTER_ROWS = 16
CHUNK = 512


def passed_along(x, axis, by):
    length = lax.axis_size(axis)
    pairs = [(i, i + by) for i in range(length) if 0 <= i + by < length]
    return lax.ppermute(x, axis, pairs)


def ring_pairs(away):
    chips = lax.axis_size("expert") // 2
    pairs = []
    for chip in range(chips):
        for core in range(2):
            step = away if core == 0 else -away
            pairs.append((2 * chip + core, 2 * ((chip + step) % chips) + core))
    return pairs


def ahead(x):
    return lax.ppermute(x, "expert", ring_pairs(1))


def behind(x):
    return lax.ppermute(x, "expert", ring_pairs(-1))


def swapped(x):
    return lax.ppermute(x, "expert", [(i, i ^ 1) for i in range(lax.axis_size("expert"))])


def gather(block):
    near = ahead(block)
    back = behind(block)
    own_other = swapped(block)
    far = ahead(near)
    near_other = swapped(near)
    back_other = swapped(back)
    far_other = swapped(far)
    return [block, own_other, near, near_other, back, back_other, far, far_other]


def scatter_sum(blocks):
    own, own_other, near, near_other, back, back_other, far, far_other = blocks

    def both(mine, other):
        return (mine.astype(jnp.float32) + swapped(other).astype(jnp.float32)).astype(jnp.bfloat16)

    far = both(far, far_other)
    passing = behind(far)
    back = both(back, back_other)
    from_back = ahead(back)
    near = near.astype(jnp.float32) + swapped(near_other).astype(jnp.float32)
    near = (near + passing.astype(jnp.float32)).astype(jnp.bfloat16)
    from_near = behind(near)
    return (
        own.astype(jnp.float32)
        + swapped(own_other).astype(jnp.float32)
        + from_back.astype(jnp.float32)
        + from_near.astype(jnp.float32)
    )


def contract_cols(first_operand, second_operand):
    return lax.dot_general(
        first_operand, second_operand, (((1,), (1,)), ((), ())), preferred_element_type=jnp.float32
    )


def stacked(blocks, columns):
    return jnp.concatenate([block[:, columns] for block in blocks], axis=0)


def over_chunks(width, chunk, step):
    def body(index, carry):
        step(index, pl.ds(pl.multiple_of(index * chunk, chunk), chunk))
        return carry

    lax.fori_loop(0, width // chunk, body, 0)


def read_side(blocks, width, experts, mine):
    columns = stacked(blocks, slice(width, width + LANES)).astype(jnp.float32)
    table = columns[:, :experts] + columns[:, experts : 2 * experts]
    lane = lax.broadcasted_iota(jnp.int32, table.shape, 1)
    weight = jnp.sum(jnp.where(lane == mine, table, 0.0), axis=1, keepdims=True)
    inverse = columns[:, 2 * experts : 2 * experts + 1] + columns[:, 2 * experts + 1 : 2 * experts + 2]
    return (table, lane, weight, inverse)


def project_kernel(owners, *refs):
    blocks, gate_up, projected = refs[:owners], refs[owners], refs[owners + 1]
    projected[...] = jnp.zeros_like(projected)

    def step(index, columns):
        projected[...] += jnp.dot(
            stacked(blocks, columns), gate_up[columns, :], preferred_element_type=jnp.float32
        )

    over_chunks(gate_up.shape[0], CHUNK, step)


def middle_kernel(owners, experts, *refs):
    mine_ref, projected_ref, down = refs[:3]
    blocks = refs[3 : 3 + owners]
    grads, steps, first_turned, second_turned, bare = refs[3 + owners :]
    hidden_width, width = down.shape
    mine = mine_ref[0]
    bare[...] = jnp.zeros_like(bare)

    def step(index, columns):
        bare[...] += contract_cols(stacked(blocks, columns), down[:, columns])

    over_chunks(width, CHUNK, step)
    table, lane, weight, inverse = read_side(blocks, width, experts, mine)
    projected = projected_ref[...] * inverse
    pre_gate = projected[:, :hidden_width]
    pre_up = projected[:, hidden_width:]
    sigmoid_gate = jax.nn.sigmoid(pre_gate)
    active = pre_gate * sigmoid_gate
    hidden = active * pre_up
    bare_grad = bare[...]
    gate_grad = jnp.sum(hidden * bare_grad, axis=1, keepdims=True)
    hidden_grad = bare_grad * weight
    grad_g = hidden_grad * pre_up * sigmoid_gate * (1.0 + pre_gate * (1.0 - sigmoid_gate))
    grad_u = hidden_grad * active
    other = jnp.sum(table, axis=1, keepdims=True) - weight
    sign = jnp.where(lane == mine, 1.0, jnp.where(table > 0.0, -1.0, 0.0))
    logit_part = weight * other * gate_grad * sign
    logit_part = jnp.concatenate(
        [logit_part, jnp.zeros((table.shape[0], LANES - experts), jnp.float32)], axis=1
    )
    grads[:, :hidden_width] = grad_g.astype(jnp.bfloat16)
    grads[:, hidden_width:] = grad_u.astype(jnp.bfloat16)
    steps[...] = logit_part.astype(jnp.bfloat16)
    first_turned[:hidden_width, :] = (grad_g * inverse).T.astype(jnp.bfloat16)
    first_turned[hidden_width : 2 * hidden_width, :] = (grad_u * inverse).T.astype(jnp.bfloat16)
    first_turned[2 * hidden_width :, :] = (logit_part * inverse).T[:ROUTER_ROWS].astype(jnp.bfloat16)
    second_turned[...] = (hidden * weight).T.astype(jnp.bfloat16)


def weights_kernel(owners, *refs):
    first_turned, second_turned = refs[:2]
    rows, ups, out = refs[2 : 2 + owners], refs[2 + owners : 2 + 2 * owners], refs[2 + 2 * owners]
    parts, height, share = out.shape
    middle = first_turned.shape[0] - ROUTER_ROWS

    def step(index, columns):
        first = jnp.dot(first_turned[...], stacked(rows, columns), preferred_element_type=jnp.float32)
        second = jnp.dot(second_turned[...], stacked(ups, columns), preferred_element_type=jnp.float32)
        out[index, :middle, :] = first[:middle].astype(jnp.bfloat16)
        out[index, middle : height - ROUTER_ROWS, :] = second.astype(jnp.bfloat16)
        out[index, height - ROUTER_ROWS :, :] = first[middle:].astype(jnp.bfloat16)

    over_chunks(parts * share, share, step)


def rows_kernel(grads, steps, gate_up, router_turned, *outs):
    tokens = outs[0].shape[0]

    def step(index, columns):
        result = contract_cols(grads[...], gate_up[columns, :])
        result += jnp.dot(steps[...], router_turned[:, columns], preferred_element_type=jnp.float32)
        for place, out in enumerate(outs):
            out[:, columns] = result[place * tokens : (place + 1) * tokens].astype(jnp.bfloat16)

    over_chunks(gate_up.shape[0], CHUNK, step)


def forward_kernel(owners, experts, *refs):
    mine_ref, gate_up, down = refs[:3]
    blocks, outs, projected_ref = refs[3 : 3 + owners], refs[3 + owners : 3 + 2 * owners], refs[-1]
    hidden_width, width = down.shape
    tokens = outs[0].shape[0]
    projected_ref[...] = jnp.zeros_like(projected_ref)

    def project(index, columns):
        projected_ref[...] += jnp.dot(
            stacked(blocks, columns), gate_up[columns, :], preferred_element_type=jnp.float32
        )

    over_chunks(width, CHUNK, project)
    table, lane, weight, inverse = read_side(blocks, width, experts, mine_ref[0])
    projected = projected_ref[...] * inverse
    pre_gate = projected[:, :hidden_width]
    pre_up = projected[:, hidden_width:]
    hidden = (pre_gate * jax.nn.sigmoid(pre_gate) * pre_up * weight).astype(jnp.bfloat16)

    def step(index, columns):
        result = jnp.dot(hidden, down[:, columns], preferred_element_type=jnp.float32)
        for place, out in enumerate(outs):
            out[:, columns] = result[place * tokens : (place + 1) * tokens].astype(jnp.bfloat16)

    over_chunks(width, CHUNK, step)


def kernel_call(kernel, name, operands, outs, flops, scratch=(), scalars=0):
    whole = pl.BlockSpec(memory_space=pltpu.VMEM)
    scalar = pl.BlockSpec(memory_space=pltpu.SMEM)
    return pl.pallas_call(
        kernel,
        name=name,
        out_shape=outs,
        in_specs=[scalar] * scalars + [whole] * (len(operands) - scalars),
        out_specs=[whole] * len(outs),
        scratch_shapes=list(scratch),
        compiler_params=pltpu.CompilerParams(vmem_limit_bytes=12 << 20),
        cost_estimate=pl.CostEstimate(flops=flops, bytes_accessed=10_000_000, transcendentals=0),
    )(*operands)


def inverse_spread(values):
    values = values.astype(jnp.float32)
    return lax.rsqrt(jnp.mean(values * values, axis=-1, keepdims=True) + EPSILON)


def gate_table(normed, router_w, routes):
    experts = router_w.shape[1]
    logits = jnp.dot(normed, router_w, preferred_element_type=jnp.float32)
    onehot = (routes[:, :, None] == jnp.arange(experts, dtype=jnp.int32)[None, None, :]).astype(
        jnp.float32
    )
    chosen = jnp.sum(onehot * logits[:, None, :], axis=2)
    first_gate = jax.nn.sigmoid(chosen[:, 0] - chosen[:, 1])
    second_gate = jax.nn.sigmoid(chosen[:, 1] - chosen[:, 0])
    table = onehot[:, 0, :] * first_gate[:, None] + onehot[:, 1, :] * second_gate[:, None]
    return (first_gate, second_gate, onehot, table)


def halves(values):
    high = lax.reduce_precision(values, exponent_bits=8, mantissa_bits=7)
    return (high.astype(jnp.bfloat16), (values - high).astype(jnp.bfloat16))


def side_columns(table, inverse):
    table_high, table_low = halves(table)
    inverse_high, inverse_low = halves(inverse)
    columns = jnp.concatenate([table_high, table_low, inverse_high, inverse_low], axis=1)
    return jnp.pad(columns, ((0, 0), (0, LANES - columns.shape[1])))


def shards(
    fresh, cotangent, prev_out, prev_grad, saved_in, route_fwd, route_bwd, router, gate_up, down
):
    section_index = lax.axis_index("pipe")
    sections = lax.axis_size("pipe")
    replicas = lax.axis_size("dp")
    owners = lax.axis_size("expert")
    mine = lax.axis_index("expert")
    inputs_bwd = saved_in[0]
    router_w = router[0]
    gate_up_w = gate_up[0, 0]
    down_w = down[0, 0]
    tokens, width = fresh.shape
    experts = router_w.shape[1]
    hidden_width = down_w.shape[0]

    returned = passed_along(prev_grad[0], "pipe", -1)
    arrived = passed_along(prev_out[0], "pipe", 1)
    rows_bwd = gather(inputs_bwd)
    inverse_bwd = inverse_spread(inputs_bwd)
    unit_bwd = inputs_bwd.astype(jnp.float32) * inverse_bwd
    first_bwd, second_bwd, onehot_bwd, table_bwd = gate_table(
        unit_bwd.astype(jnp.bfloat16), router_w, route_bwd[0]
    )
    upstream = jnp.where(section_index == sections - 1, cotangent, returned)
    ups = gather(jnp.concatenate([upstream, side_columns(table_bwd, inverse_bwd)], axis=1))

    inputs_fwd = jnp.where(section_index == 0, fresh, arrived)
    inverse_fwd = inverse_spread(inputs_fwd)
    normed_fwd = (inputs_fwd.astype(jnp.float32) * inverse_fwd).astype(jnp.bfloat16)
    table_fwd = gate_table(normed_fwd, router_w, route_fwd[0])[3]
    sent_fwd = jnp.concatenate([inputs_fwd, side_columns(table_fwd, inverse_fwd)], axis=1)
    sent_fwd, far_up = lax.optimization_barrier((sent_fwd, ups[6]))
    ups = [*ups[:6], far_up, ups[7]]
    rows_fwd = gather(sent_fwd)

    count = owners * tokens
    share = width // replicas
    scalar = mine.astype(jnp.int32).reshape(1)
    router_turned = jnp.pad(router_w.T, ((0, LANES - experts), (0, 0)))
    block_shape = jax.ShapeDtypeStruct((tokens, width), jnp.bfloat16)
    flops = 2 * count * width * hidden_width
    (projected,) = kernel_call(
        functools.partial(project_kernel, owners),
        "project",
        (*rows_bwd, gate_up_w),
        [jax.ShapeDtypeStruct((count, 2 * hidden_width), jnp.float32)],
        2 * flops,
    )
    grads, steps, first_turned, second_turned = kernel_call(
        functools.partial(middle_kernel, owners, experts),
        "middle",
        (scalar, projected, down_w, *ups),
        [
            jax.ShapeDtypeStruct((count, 2 * hidden_width), jnp.bfloat16),
            jax.ShapeDtypeStruct((count, LANES), jnp.bfloat16),
            jax.ShapeDtypeStruct((2 * hidden_width + ROUTER_ROWS, count), jnp.bfloat16),
            jax.ShapeDtypeStruct((hidden_width, count), jnp.bfloat16),
        ],
        flops,
        [pltpu.VMEM((count, hidden_width), jnp.float32)],
        1,
    )
    height = 3 * hidden_width + ROUTER_ROWS
    (weight_parts,) = kernel_call(
        functools.partial(weights_kernel, owners),
        "weights",
        (first_turned, second_turned, *rows_bwd, *ups),
        [jax.ShapeDtypeStruct((replicas, height, share), jnp.bfloat16)],
        3 * flops,
    )
    weight_sums = lax.psum_scatter(weight_parts, "dp", scatter_dimension=0, tiled=True)[0]
    back_blocks = kernel_call(
        rows_kernel,
        "rows",
        (grads, steps, gate_up_w, router_turned),
        [block_shape] * owners,
        2 * flops,
    )
    out_blocks = kernel_call(
        functools.partial(forward_kernel, owners, experts),
        "forward",
        (scalar, gate_up_w, down_w, *rows_fwd),
        [block_shape] * owners,
        3 * flops,
        [pltpu.VMEM((count, 2 * hidden_width), jnp.float32)],
        1,
    )
    normed_grad = scatter_sum(back_blocks)
    inner_mean = jnp.mean(normed_grad * unit_bwd, axis=1, keepdims=True)
    grad_value = upstream.astype(jnp.float32) + (normed_grad - unit_bwd * inner_mean) * inverse_bwd
    input_grad = grad_value.astype(jnp.bfloat16)
    section_out = (inputs_fwd.astype(jnp.float32) + scatter_sum(out_blocks)).astype(jnp.bfloat16)

    grad_gate_up = weight_sums[: 2 * hidden_width].T
    grad_down = weight_sums[2 * hidden_width : 3 * hidden_width]
    router_sum = weight_sums[3 * hidden_width : 3 * hidden_width + experts].astype(jnp.float32)
    bit = 1
    while bit < owners:
        router_sum = router_sum + lax.ppermute(
            router_sum, "expert", [(i, i ^ bit) for i in range(owners)]
        )
        bit = 2 * bit
    piece = share // owners
    router_sum = router_sum.reshape(experts, owners, piece)
    pick = (jnp.arange(owners, dtype=jnp.int32) == mine).astype(jnp.float32)[None, :, None]
    grad_router = jnp.sum(router_sum * pick, axis=1).T
    return (
        section_out[None],
        input_grad[None],
        grad_gate_up[None, None],
        grad_down[None, None],
        grad_router[None],
    )


def solution(mesh):
    placed = (
        P(("dp", "expert"), None),
        P(("dp", "expert"), None),
        P("pipe", ("dp", "expert"), None),
        P("pipe", ("dp", "expert"), None),
        P("pipe", ("dp", "expert"), None),
        P("pipe", ("dp", "expert"), None),
        P("pipe", ("dp", "expert"), None),
        P("pipe", None, None),
        P("pipe", "expert", None, None),
        P("pipe", "expert", None, None),
    )
    return jax.shard_map(
        shards,
        mesh=mesh,
        in_specs=placed,
        out_specs=(
            P("pipe", ("dp", "expert"), None),
            P("pipe", ("dp", "expert"), None),
            P("pipe", "expert", "dp", None),
            P("pipe", "expert", None, "dp"),
            P("pipe", ("dp", "expert"), None),
        ),
        check_vma=False,
    )
```

```python
import functools

import jax
import jax.numpy as jnp
from jax import lax
from jax.experimental import pallas as pl
from jax.experimental.pallas import tpu as pltpu
from jax.sharding import PartitionSpec as P


EPSILON = 1e-05
LANES = 128
ROUTER_ROWS = 16
CHUNK = 512


def passed_along(x, axis, by):
    length = lax.axis_size(axis)
    pairs = [(i, i + by) for i in range(length) if 0 <= i + by < length]
    return lax.ppermute(x, axis, pairs)


def ring_pairs(away):
    chips = lax.axis_size("expert") // 2
    pairs = []
    for chip in range(chips):
        for core in range(2):
            step = away if core == 0 else -away
            pairs.append((2 * chip + core, 2 * ((chip + step) % chips) + core))
    return pairs


def ahead(x):
    return lax.ppermute(x, "expert", ring_pairs(1))


def behind(x):
    return lax.ppermute(x, "expert", ring_pairs(-1))


def swapped(x):
    return lax.ppermute(x, "expert", [(i, i ^ 1) for i in range(lax.axis_size("expert"))])


def gather(block):
    near = ahead(block)
    back = behind(block)
    own_other = swapped(block)
    far = ahead(near)
    near_other = swapped(near)
    back_other = swapped(back)
    far_other = swapped(far)
    return [block, own_other, near, near_other, back, back_other, far, far_other]


def scatter_sum(blocks):
    own, own_other, near, near_other, back, back_other, far, far_other = blocks

    def both(mine, other):
        other = swapped(other)
        return mine.astype(jnp.float32) + other.astype(jnp.float32)

    far = both(far, far_other).astype(jnp.bfloat16)
    passing = behind(far)
    back = both(back, back_other).astype(jnp.bfloat16)
    from_back = ahead(back)
    near = both(near, near_other)
    near = (near + passing.astype(jnp.float32)).astype(jnp.bfloat16)
    from_near = behind(near)
    own = both(own, own_other)
    return own + from_back.astype(jnp.float32) + from_near.astype(jnp.float32)


def contract_cols(first_operand, second_operand):
    return lax.dot_general(
        first_operand, second_operand, (((1,), (1,)), ((), ())), preferred_element_type=jnp.float32
    )


def stacked(blocks, columns):
    return jnp.concatenate([block[:, columns] for block in blocks], axis=0)


def over_chunks(width, chunk, step):
    def body(index, carry):
        step(index, pl.ds(pl.multiple_of(index * chunk, chunk), chunk))
        return carry

    lax.fori_loop(0, width // chunk, body, 0)


def read_side(blocks, width, experts, mine):
    columns = stacked(blocks, slice(width, width + LANES)).astype(jnp.float32)
    table = columns[:, :experts] + columns[:, experts : 2 * experts]
    lane = lax.broadcasted_iota(jnp.int32, table.shape, 1)
    weight = jnp.sum(jnp.where(lane == mine, table, 0.0), axis=1, keepdims=True)
    inverse = columns[:, 2 * experts : 2 * experts + 1] + columns[:, 2 * experts + 1 : 2 * experts + 2]
    return (table, lane, weight, inverse)


def project_kernel(owners, *refs):
    blocks, gate_up, projected = refs[:owners], refs[owners], refs[owners + 1]
    projected[...] = jnp.zeros_like(projected)

    def step(index, columns):
        projected[...] += jnp.dot(
            stacked(blocks, columns), gate_up[columns, :], preferred_element_type=jnp.float32
        )

    over_chunks(gate_up.shape[0], CHUNK, step)


def middle_kernel(owners, experts, first_row, *refs):
    mine_ref, projected_ref, down = refs[:3]
    blocks = refs[3 : 3 + owners]
    grads, steps, first_turned, second_turned, bare = refs[3 + owners :]
    hidden_width, width = down.shape
    count = grads.shape[0]
    mine = mine_ref[0]
    bare[...] = jnp.zeros_like(bare)

    def step(index, columns):
        bare[...] += contract_cols(stacked(blocks, columns), down[:, columns])

    over_chunks(width, CHUNK, step)
    table, lane, weight, inverse = read_side(blocks, width, experts, mine)
    projected = projected_ref[first_row : first_row + count, :] * inverse
    pre_gate = projected[:, :hidden_width]
    pre_up = projected[:, hidden_width:]
    sigmoid_gate = jax.nn.sigmoid(pre_gate)
    active = pre_gate * sigmoid_gate
    hidden = active * pre_up
    bare_grad = bare[...]
    gate_grad = jnp.sum(hidden * bare_grad, axis=1, keepdims=True)
    hidden_grad = bare_grad * weight
    grad_g = hidden_grad * pre_up * sigmoid_gate * (1.0 + pre_gate * (1.0 - sigmoid_gate))
    grad_u = hidden_grad * active
    other = jnp.sum(table, axis=1, keepdims=True) - weight
    sign = jnp.where(lane == mine, 1.0, jnp.where(table > 0.0, -1.0, 0.0))
    logit_part = weight * other * gate_grad * sign
    logit_part = jnp.concatenate(
        [logit_part, jnp.zeros((count, LANES - experts), jnp.float32)], axis=1
    )
    grads[:, :hidden_width] = grad_g.astype(jnp.bfloat16)
    grads[:, hidden_width:] = grad_u.astype(jnp.bfloat16)
    steps[...] = logit_part.astype(jnp.bfloat16)
    first_turned[:hidden_width, :] = (grad_g * inverse).T.astype(jnp.bfloat16)
    first_turned[hidden_width : 2 * hidden_width, :] = (grad_u * inverse).T.astype(jnp.bfloat16)
    first_turned[2 * hidden_width :, :] = (logit_part * inverse).T[:ROUTER_ROWS].astype(jnp.bfloat16)
    second_turned[...] = (hidden * weight).T.astype(jnp.bfloat16)


def weights_kernel(owners, shifts, replicas, *refs):
    replica_ref, turned, refs = refs[0], refs[1:5], refs[5:]
    rows, ups = refs[:owners], refs[owners : 2 * owners]
    left_out, right_out = refs[2 * owners :]
    left, share = left_out.shape[1:]
    middle = turned[0].shape[0] - ROUTER_ROWS
    extra = middle - left
    replica = replica_ref[0]
    first_shift, count, wrap = shifts

    def body(index, carry):
        shift = jnp.where(index == count - 1, wrap, index + first_shift)
        columns = pl.ds(pl.multiple_of(((replica + replicas - shift) % replicas) * share, share), share)
        first = jnp.dot(
            jnp.concatenate([turned[0][...], turned[1][...]], axis=1),
            stacked(rows, columns),
            preferred_element_type=jnp.float32,
        )
        second = jnp.dot(
            jnp.concatenate([turned[2][...], turned[3][...]], axis=1),
            stacked(ups, columns),
            preferred_element_type=jnp.float32,
        )
        height = second.shape[0]
        mirror = jnp.where(index == count - 1, index, count - 2 - index)
        if wrap:
            mirror = count - 1 - index
        left_out[index] = first[:left].astype(jnp.bfloat16)
        right_out[mirror, :extra, :] = first[left:middle].astype(jnp.bfloat16)
        right_out[mirror, extra : extra + height, :] = second.astype(jnp.bfloat16)
        right_out[mirror, extra + height :, :] = first[middle:].astype(jnp.bfloat16)
        return carry

    lax.fori_loop(0, count, body, 0)


def rows_kernel(grads, steps, gate_up, router_turned, *outs):
    tokens = outs[0].shape[0]

    def step(index, columns):
        result = contract_cols(grads[...], gate_up[columns, :])
        result += jnp.dot(steps[...], router_turned[:, columns], preferred_element_type=jnp.float32)
        for place, out in enumerate(outs):
            out[:, columns] = result[place * tokens : (place + 1) * tokens].astype(jnp.bfloat16)

    over_chunks(gate_up.shape[0], CHUNK, step)


def forward_kernel(owners, experts, *refs):
    mine_ref, gate_up, down = refs[:3]
    blocks, outs, projected_ref = refs[3 : 3 + owners], refs[3 + owners : 3 + 2 * owners], refs[-1]
    hidden_width, width = down.shape
    tokens = outs[0].shape[0]
    projected_ref[...] = jnp.zeros_like(projected_ref)

    def project(index, columns):
        projected_ref[...] += jnp.dot(
            stacked(blocks, columns), gate_up[columns, :], preferred_element_type=jnp.float32
        )

    over_chunks(width, CHUNK, project)
    _, _, weight, inverse = read_side(blocks, width, experts, mine_ref[0])
    projected = projected_ref[...] * inverse
    pre_gate = projected[:, :hidden_width]
    pre_up = projected[:, hidden_width:]
    hidden = (pre_gate * jax.nn.sigmoid(pre_gate) * pre_up * weight).astype(jnp.bfloat16)

    def step(index, columns):
        result = jnp.dot(hidden, down[:, columns], preferred_element_type=jnp.float32)
        for place, out in enumerate(outs):
            out[:, columns] = result[place * tokens : (place + 1) * tokens].astype(jnp.bfloat16)

    over_chunks(width, CHUNK, step)


def kernel_call(kernel, operands, outs, flops, scratch=(), scalars=0):
    whole = pl.BlockSpec(memory_space=pltpu.VMEM)
    scalar = pl.BlockSpec(memory_space=pltpu.SMEM)
    return pl.pallas_call(
        kernel,
        out_shape=outs,
        in_specs=[scalar] * scalars + [whole] * (len(operands) - scalars),
        out_specs=[whole] * len(outs),
        scratch_shapes=list(scratch),
        compiler_params=pltpu.CompilerParams(vmem_limit_bytes=12 << 20),
        cost_estimate=pl.CostEstimate(flops=flops, bytes_accessed=10_000_000, transcendentals=0),
    )(*operands)


def inverse_spread(values):
    values = values.astype(jnp.float32)
    return lax.rsqrt(jnp.mean(values * values, axis=-1, keepdims=True) + EPSILON)


def gate_pair(normed, router_w, routes):
    experts = router_w.shape[1]
    logits = jnp.dot(normed, router_w, preferred_element_type=jnp.float32)
    onehot = (routes[:, :, None] == jnp.arange(experts, dtype=jnp.int32)[None, None, :]).astype(
        jnp.float32
    )
    chosen = jnp.sum(onehot * logits[:, None, :], axis=2)
    return (
        jax.nn.sigmoid(chosen[:, 0:1] - chosen[:, 1:2]),
        jax.nn.sigmoid(chosen[:, 1:2] - chosen[:, 0:1]),
    )


def side_columns(gates, routes, inverse, experts):
    lane = jnp.arange(LANES, dtype=jnp.int32)[None, :]
    places = (routes[:, 0:1], routes[:, 1:2], jnp.full_like(routes[:, 0:1], 2 * experts))
    low_shift = (experts, experts, 1)
    total = jnp.zeros((routes.shape[0], LANES), jnp.float32)
    for value, place, shift in zip((*gates, inverse), places, low_shift):
        high = lax.reduce_precision(value, exponent_bits=8, mantissa_bits=7)
        total += jnp.where(lane == place, high, 0.0)
        total += jnp.where(lane == place + shift, value - high, 0.0)
    return total.astype(jnp.bfloat16)


def section_step(
    fresh, cotangent, prev_out, prev_grad, saved_in, route_fwd, route_bwd, router, gate_up, down
):
    section_index = lax.axis_index("pipe")
    sections = lax.axis_size("pipe")
    replicas = lax.axis_size("dp")
    owners = lax.axis_size("expert")
    mine = lax.axis_index("expert")
    inputs_bwd = saved_in[0]
    router_w = router[0]
    gate_up_w = gate_up[0, 0]
    down_w = down[0, 0]
    tokens, width = fresh.shape
    experts = router_w.shape[1]
    hidden_width = down_w.shape[0]

    rows_bwd = gather(inputs_bwd)
    returned = passed_along(prev_grad[0], "pipe", -1)
    arrived = passed_along(prev_out[0], "pipe", 1)
    inverse_bwd = inverse_spread(inputs_bwd)
    unit_bwd = inputs_bwd.astype(jnp.float32) * inverse_bwd
    gates = gate_pair(unit_bwd.astype(jnp.bfloat16), router_w, route_bwd[0])
    upstream = jnp.where(section_index == sections - 1, cotangent, returned)
    side = side_columns(gates, route_bwd[0], inverse_bwd, experts)
    ups = gather(jnp.concatenate([upstream, side], axis=1))

    inputs_fwd = jnp.where(section_index == 0, fresh, arrived)
    inverse_fwd = inverse_spread(inputs_fwd)
    normed_fwd = (inputs_fwd.astype(jnp.float32) * inverse_fwd).astype(jnp.bfloat16)
    gates = gate_pair(normed_fwd, router_w, route_fwd[0])
    side = side_columns(gates, route_fwd[0], inverse_fwd, experts)
    rows_fwd = gather(jnp.concatenate([inputs_fwd, side], axis=1))

    count = owners * tokens
    share = width // replicas
    scalar = mine.astype(jnp.int32).reshape(1)
    router_turned = jnp.pad(router_w.T, ((0, LANES - experts), (0, 0)))
    block_shape = jax.ShapeDtypeStruct((tokens, width), jnp.bfloat16)
    flops = 2 * count * width * hidden_width
    (projected,) = kernel_call(
        functools.partial(project_kernel, owners),
        (*rows_bwd, gate_up_w),
        [jax.ShapeDtypeStruct((count, 2 * hidden_width), jnp.float32)],
        2 * flops,
    )
    early = owners - 2

    def middle(first, last):
        size = (last - first) * tokens
        return kernel_call(
            functools.partial(middle_kernel, last - first, experts, first * tokens),
            (scalar, projected, down_w, *ups[first:last]),
            [
                jax.ShapeDtypeStruct((size, 2 * hidden_width), jnp.bfloat16),
                jax.ShapeDtypeStruct((size, LANES), jnp.bfloat16),
                jax.ShapeDtypeStruct((2 * hidden_width + ROUTER_ROWS, size), jnp.bfloat16),
                jax.ShapeDtypeStruct((hidden_width, size), jnp.bfloat16),
            ],
            flops * (last - first) // owners,
            [pltpu.VMEM((size, hidden_width), jnp.float32)],
            1,
        )

    left = 3 * hidden_width // 2
    right = 3 * hidden_width - left + ROUTER_ROWS
    place = lax.axis_index("dp").astype(jnp.int32).reshape(1)

    def weights(shifts):
        _, number, _ = shifts
        return kernel_call(
            functools.partial(weights_kernel, owners, shifts, replicas),
            (place, early_first, late_first, early_second, late_second, *rows_bwd, *ups),
            [
                jax.ShapeDtypeStruct((number, left, share), jnp.bfloat16),
                jax.ShapeDtypeStruct((number, right, share), jnp.bfloat16),
            ],
            3 * flops * number // replicas,
            (),
            1,
        )

    def rows(grads, steps, number):
        return kernel_call(
            rows_kernel,
            (grads, steps, gate_up_w, router_turned),
            [block_shape] * number,
            2 * flops * number // owners,
        )

    def forward(first, last):
        size = (last - first) * tokens
        return kernel_call(
            functools.partial(forward_kernel, last - first, experts),
            (scalar, gate_up_w, down_w, *rows_fwd[first:last]),
            [block_shape] * (last - first),
            3 * flops * (last - first) // owners,
            [pltpu.VMEM((size, 2 * hidden_width), jnp.float32)],
            1,
        )

    early_grads, early_steps, early_first, early_second = middle(0, early)
    late_grads, late_steps, late_first, late_second = middle(early, owners)
    left_ends, right_ends = weights((1, 2, replicas - 1))
    late_grads, left_ends, right_ends = lax.optimization_barrier((late_grads, left_ends, right_ends))
    late_back = rows(late_grads, late_steps, 2)
    early_first, late_back = lax.optimization_barrier((early_first, late_back))
    left_rest, right_rest = weights((2, replicas - 2, 0))
    early_grads, left_rest, right_rest = lax.optimization_barrier((early_grads, left_rest, right_rest))
    early_back = rows(early_grads, early_steps, early)
    back_blocks = [*early_back, *late_back]
    out_blocks = [*forward(0, early), *forward(early, owners)]

    def ring_sum(ends, rest, away):
        pairs = [(i, (i + away) % replicas) for i in range(replicas)]
        running = ends[0]
        for hop in range(1, replicas + 1):
            if hop > 1:
                term = ends[1] if hop == replicas - 1 else rest[hop - 2 - (hop == replicas)]
                running = (moved.astype(jnp.float32) + term.astype(jnp.float32)).astype(jnp.bfloat16)
            if hop < replicas:
                moved = lax.ppermute(running, "dp", pairs)
        return running

    left_sum = ring_sum(left_ends, left_rest, 1)
    right_sum = ring_sum(right_ends, right_rest, -1)
    normed_grad = scatter_sum(back_blocks)
    inner_mean = jnp.mean(normed_grad * unit_bwd, axis=1, keepdims=True)
    grad_value = upstream.astype(jnp.float32) + (normed_grad - unit_bwd * inner_mean) * inverse_bwd
    input_grad = grad_value.astype(jnp.bfloat16)
    back_fwd = scatter_sum(out_blocks)
    section_out = (inputs_fwd.astype(jnp.float32) + back_fwd).astype(jnp.bfloat16)

    extra = 2 * hidden_width - left
    grad_gate_up = jnp.concatenate([left_sum.T, right_sum[:extra].T], axis=1)
    grad_down = right_sum[extra : extra + hidden_width]
    router_sum = right_sum[extra + hidden_width : extra + hidden_width + experts].astype(jnp.float32)
    bit = 1
    while bit < owners:
        router_sum = router_sum + lax.ppermute(
            router_sum, "expert", [(i, i ^ bit) for i in range(owners)]
        )
        bit = 2 * bit
    piece = share // owners
    wanted = jnp.arange(piece, dtype=jnp.int32)[None, :] + mine * piece
    pick = (jnp.arange(share, dtype=jnp.int32)[:, None] == wanted).astype(jnp.float32)
    grad_router = lax.dot_general(
        pick,
        router_sum,
        (((0,), (1,)), ((), ())),
        precision=lax.Precision.HIGHEST,
        preferred_element_type=jnp.float32,
    )
    return (
        section_out[None],
        input_grad[None],
        grad_gate_up[None, None],
        grad_down[None, None],
        grad_router[None],
    )


def solution(mesh):
    placed = (
        P(("dp", "expert"), None),
        P(("dp", "expert"), None),
        P("pipe", ("dp", "expert"), None),
        P("pipe", ("dp", "expert"), None),
        P("pipe", ("dp", "expert"), None),
        P("pipe", ("dp", "expert"), None),
        P("pipe", ("dp", "expert"), None),
        P("pipe", None, None),
        P("pipe", "expert", None, None),
        P("pipe", "expert", None, None),
    )
    return jax.shard_map(
        section_step,
        mesh=mesh,
        in_specs=placed,
        out_specs=(
            P("pipe", ("dp", "expert"), None),
            P("pipe", ("dp", "expert"), None),
            P("pipe", "expert", "dp", None),
            P("pipe", "expert", None, "dp"),
            P("pipe", ("dp", "expert"), None),
        ),
        check_vma=False,
    )
```

```python
import functools

import jax
import jax.numpy as jnp
from jax import lax
from jax.experimental import pallas as pl
from jax.experimental.pallas import tpu as pltpu
from jax.sharding import PartitionSpec as P


EPSILON = 1e-05
LANES = 128
ROUTER_ROWS = 16
CHUNK = 256


def passed_along(x, axis, by):
    length = lax.axis_size(axis)
    pairs = [(i, i + by) for i in range(length) if 0 <= i + by < length]
    return lax.ppermute(x, axis, pairs)


def ring_pairs(away):
    chips = lax.axis_size("expert") // 2
    pairs = []
    for chip in range(chips):
        for core in range(2):
            step = away if core == 0 else -away
            pairs.append((2 * chip + core, 2 * ((chip + step) % chips) + core))
    return pairs


def ahead(x):
    return lax.ppermute(x, "expert", ring_pairs(1))


def behind(x):
    return lax.ppermute(x, "expert", ring_pairs(-1))


def swapped(x):
    return lax.ppermute(x, "expert", [(i, i ^ 1) for i in range(lax.axis_size("expert"))])


def gather(block):
    near = ahead(block)
    back = behind(block)
    own_other = swapped(block)
    far = ahead(near)
    near_other = swapped(near)
    back_other = swapped(back)
    far_other = swapped(far)
    return [block, own_other, near, near_other, back, back_other, far, far_other]


def scatter_sum(mine, far_other, back_other, others):
    own, near, back, far = mine
    tokens = own.shape[0]

    def wide(x):
        return x.astype(jnp.float32)

    far_other = swapped(far_other)
    back_other = swapped(back_other)
    others = swapped(others)
    far = (wide(far) + wide(far_other)).astype(jnp.bfloat16)
    passing = behind(far)
    back = (wide(back) + wide(back_other)).astype(jnp.bfloat16)
    from_back = ahead(back)
    near = (wide(near) + wide(others[:tokens]) + wide(passing)).astype(jnp.bfloat16)
    from_near = behind(near)
    return wide(own) + wide(others[tokens:]) + wide(from_back) + wide(from_near)


def contract_cols(first_operand, second_operand):
    return lax.dot_general(
        first_operand, second_operand, (((1,), (1,)), ((), ())), preferred_element_type=jnp.float32
    )


def stacked(blocks, columns):
    return jnp.concatenate([block[:, columns] for block in blocks], axis=0)


def over_chunks(width, chunk, step):
    def body(index, carry):
        step(index, pl.ds(pl.multiple_of(index * chunk, chunk), chunk))
        return carry

    lax.fori_loop(0, width // chunk, body, 0)


def over_rows(count, step):
    def body(index, carry):
        step(pl.ds(pl.multiple_of(index * LANES, LANES), LANES))
        return carry

    lax.fori_loop(0, count // LANES, body, 0)


def read_side(columns, experts, mine):
    table = columns[:, :experts] + columns[:, experts : 2 * experts]
    lane = lax.broadcasted_iota(jnp.int32, table.shape, 1)
    weight = jnp.sum(jnp.where(lane == mine, table, 0.0), axis=1, keepdims=True)
    inverse = columns[:, 2 * experts : 2 * experts + 1] + columns[:, 2 * experts + 1 : 2 * experts + 2]
    return (table, lane, weight, inverse)


def project_kernel(owners, *refs):
    blocks, gate_up, projected = refs[:owners], refs[owners], refs[owners + 1]
    projected[...] = jnp.zeros_like(projected)

    def step(index, columns):
        projected[...] += jnp.dot(
            stacked(blocks, columns), gate_up[columns, :], preferred_element_type=jnp.float32
        )

    over_chunks(gate_up.shape[0], CHUNK, step)


def middle_kernel(owners, experts, first_row, *refs):
    mine_ref, projected_ref, down = refs[:3]
    blocks = refs[3 : 3 + owners]
    grads, steps, first_turned, second_turned, bare, side = refs[3 + owners :]
    hidden_width, width = down.shape
    count = grads.shape[0]
    mine = mine_ref[0]
    bare[...] = jnp.zeros_like(bare)
    side[...] = stacked(blocks, slice(width, width + LANES)).astype(jnp.float32)

    def step(index, columns):
        bare[...] += contract_cols(stacked(blocks, columns), down[:, columns])

    over_chunks(width, CHUNK, step)

    def finish(rows):
        table, lane, weight, inverse = read_side(side[rows, :], experts, mine)
        projected = projected_ref[pl.ds(rows.start + first_row, LANES), :] * inverse
        pre_gate = projected[:, :hidden_width]
        pre_up = projected[:, hidden_width:]
        sigmoid_gate = jax.nn.sigmoid(pre_gate)
        active = pre_gate * sigmoid_gate
        hidden = active * pre_up
        bare_grad = bare[rows, :]
        gate_grad = jnp.sum(hidden * bare_grad, axis=1, keepdims=True)
        hidden_grad = bare_grad * weight
        grad_g = hidden_grad * pre_up * sigmoid_gate * (1.0 + pre_gate * (1.0 - sigmoid_gate))
        grad_u = hidden_grad * active
        other = jnp.sum(table, axis=1, keepdims=True) - weight
        sign = jnp.where(lane == mine, 1.0, jnp.where(table > 0.0, -1.0, 0.0))
        logit_part = weight * other * gate_grad * sign
        logit_part = jnp.concatenate(
            [logit_part, jnp.zeros((LANES, LANES - experts), jnp.float32)], axis=1
        )
        grads[rows, :hidden_width] = grad_g.astype(jnp.bfloat16)
        grads[rows, hidden_width:] = grad_u.astype(jnp.bfloat16)
        steps[rows, :] = logit_part.astype(jnp.bfloat16)
        first_turned[:hidden_width, rows] = (grad_g * inverse).T.astype(jnp.bfloat16)
        first_turned[hidden_width : 2 * hidden_width, rows] = (grad_u * inverse).T.astype(jnp.bfloat16)
        first_turned[2 * hidden_width :, rows] = (logit_part * inverse).T[:ROUTER_ROWS].astype(
            jnp.bfloat16
        )
        second_turned[:, rows] = (hidden * weight).T.astype(jnp.bfloat16)

    over_rows(count, finish)


def weights_kernel(owners, *refs):
    replica_ref, turned, refs = refs[0], refs[1:5], refs[5:]
    rows, ups = refs[:owners], refs[owners : 2 * owners]
    left_out, right_out, router_out = refs[2 * owners :]
    _, share = left_out.shape[1:]
    replicas = left_out.shape[0] + right_out.shape[0]
    lefts = left_out.shape[0]
    middle = turned[0].shape[0] - ROUTER_ROWS
    experts = router_out.shape[0] // replicas
    replica = replica_ref[0]

    def chunk(shift, carry):
        target = (replica + shift) % replicas

        def part(index, inner):
            first_column = pl.multiple_of(index * CHUNK, CHUNK)
            columns = pl.ds(pl.multiple_of(target * share, CHUNK) + first_column, CHUNK)
            here = pl.ds(first_column, CHUNK)
            first = jnp.dot(
                jnp.concatenate([turned[0][...], turned[1][...]], axis=1),
                stacked(rows, columns),
                preferred_element_type=jnp.float32,
            )
            second = jnp.dot(
                jnp.concatenate([turned[2][...], turned[3][...]], axis=1),
                stacked(ups, columns),
                preferred_element_type=jnp.float32,
            )

            def put(out, slot):
                out[slot, :middle, here] = first[:middle].astype(jnp.bfloat16)
                out[slot, middle:, here] = second.astype(jnp.bfloat16)

            @pl.when(shift < lefts)
            def _():
                put(left_out, shift)

            @pl.when(shift >= lefts)
            def _():
                put(right_out, shift - lefts)

            line = pl.ds(pl.multiple_of((target ^ replica) * experts, experts), experts)
            router_out[line, here] = first[middle : middle + experts]
            return inner

        return lax.fori_loop(0, share // CHUNK, part, carry)

    lax.fori_loop(0, replicas, chunk, 0)


def store_rows(result, columns, mine, far_other, back_other, others, first, tokens):
    places = [(mine[0], 0), (others, 1), (mine[1], 0), (others, 0), (mine[2], 0), (back_other, 0)]
    places = [*places, (mine[3], 0), (far_other, 0)]
    for index in range(result.shape[0] // tokens):
        out, slot = places[first + index]
        rows = slice(slot * tokens, (slot + 1) * tokens)
        out[rows, columns] = result[index * tokens : (index + 1) * tokens].astype(jnp.bfloat16)


def rows_kernel(owners, *refs):
    mine_ref, early_grads, late_grads, early_steps, late_steps, gate_up, router_turned, router_part = refs[:8]
    own, near, back, far, far_other, back_other, others, side = refs[8:]
    mine_refs = (own, near, back, far)
    tokens = own.shape[0]
    width = gate_up.shape[0]
    lines, share = router_part.shape
    piece = share // owners

    def step(index, columns):
        result = contract_cols(
            jnp.concatenate([early_grads[...], late_grads[...]], axis=0), gate_up[columns, :]
        )
        result += jnp.dot(
            jnp.concatenate([early_steps[...], late_steps[...]], axis=0),
            router_turned[:, columns],
            preferred_element_type=jnp.float32,
        )
        store_rows(result, columns, mine_refs, far_other, back_other, others, 0, tokens)

    over_chunks(width, CHUNK, step)
    me = mine_ref[0]
    chips = owners // 2
    chip, core = me // 2, me % 2
    way = 1 - 2 * core
    part = router_part[...].astype(jnp.bfloat16)
    row = lax.broadcasted_iota(jnp.int32, (share, LANES), 0)
    lane = lax.broadcasted_iota(jnp.int32, (share, LANES), 1)
    side[...] = jnp.zeros_like(side)

    def block(index, carry):
        pair, crossed = index // 2, index % 2
        back_way = way * (1 - 2 * crossed)
        move = jnp.where(pair == 1, -back_way, jnp.where(pair == 2, back_way, jnp.where(pair == 3, 2, 0)))
        owner = 2 * ((chip + move + chips) % chips) + jnp.where(crossed == 1, 1 - core, core)
        hot = jnp.where((row == owner * piece + lane) & (lane < piece), 1.0, 0.0).astype(jnp.bfloat16)
        block_rows = pl.ds(pl.multiple_of(index * tokens, tokens), lines)
        side[block_rows, :] = jnp.dot(part, hot, preferred_element_type=jnp.float32)
        return carry

    lax.fori_loop(0, owners, block, 0)
    store_rows(
        side[...],
        slice(width, width + LANES),
        mine_refs,
        far_other,
        back_other,
        others,
        0,
        tokens,
    )


def forward_kernel(owners, experts, first, *refs):
    mine_ref, gate_up, down = refs[:3]
    blocks, outs = refs[3 : 3 + owners], refs[3 + owners : -3]
    projected_ref, side, hidden_ref = refs[-3:]
    hidden_width, width = down.shape
    tokens = blocks[0].shape[0]
    projected_ref[...] = jnp.zeros_like(projected_ref)

    def project(index, columns):
        projected_ref[...] += jnp.dot(
            stacked(blocks, columns), gate_up[columns, :], preferred_element_type=jnp.float32
        )

    over_chunks(width, CHUNK, project)
    side[...] = stacked(blocks, slice(width, width + LANES)).astype(jnp.float32)

    def finish(rows):
        _, _, weight, inverse = read_side(side[rows, :], experts, mine_ref[0])
        projected = projected_ref[rows, :] * inverse
        pre_gate = projected[:, :hidden_width]
        pre_up = projected[:, hidden_width:]
        hidden_ref[rows, :] = (pre_gate * jax.nn.sigmoid(pre_gate) * pre_up * weight).astype(jnp.bfloat16)

    over_rows(side.shape[0], finish)
    if first:
        mine, far_other, back_other, others = (None, None, None, outs[0]), outs[1], None, None
    else:
        mine, far_other, back_other, others = (*outs[:3], None), None, outs[3], outs[4]

    def step(index, columns):
        result = jnp.dot(hidden_ref[...], down[:, columns], preferred_element_type=jnp.float32)
        store_rows(result, columns, mine, far_other, back_other, others, first, tokens)

    over_chunks(width, CHUNK, step)


def kernel_call(kernel, operands, outs, flops, scratch=(), scalars=0):
    whole = pl.BlockSpec(memory_space=pltpu.VMEM)
    scalar = pl.BlockSpec(memory_space=pltpu.SMEM)
    return pl.pallas_call(
        kernel,
        out_shape=outs,
        in_specs=[scalar] * scalars + [whole] * (len(operands) - scalars),
        out_specs=[whole] * len(outs),
        scratch_shapes=list(scratch),
        compiler_params=pltpu.CompilerParams(vmem_limit_bytes=12 << 20),
        cost_estimate=pl.CostEstimate(flops=flops, bytes_accessed=10_000_000, transcendentals=0),
    )(*operands)


def inverse_spread(values):
    values = values.astype(jnp.float32)
    return lax.rsqrt(jnp.mean(values * values, axis=-1, keepdims=True) + EPSILON)


def gate_pair(normed, router_w, routes):
    experts = router_w.shape[1]
    logits = jnp.dot(normed, router_w, preferred_element_type=jnp.float32)
    onehot = (routes[:, :, None] == jnp.arange(experts, dtype=jnp.int32)[None, None, :]).astype(
        jnp.float32
    )
    chosen = jnp.sum(onehot * logits[:, None, :], axis=2)
    return (
        jax.nn.sigmoid(chosen[:, 0:1] - chosen[:, 1:2]),
        jax.nn.sigmoid(chosen[:, 1:2] - chosen[:, 0:1]),
    )


def side_columns(gates, routes, inverse, experts):
    lane = jnp.arange(LANES, dtype=jnp.int32)[None, :]
    places = (routes[:, 0:1], routes[:, 1:2], jnp.full_like(routes[:, 0:1], 2 * experts))
    low_shift = (experts, experts, 1)
    total = jnp.zeros((routes.shape[0], LANES), jnp.float32)
    for value, place, shift in zip((*gates, inverse), places, low_shift):
        high = lax.reduce_precision(value, exponent_bits=8, mantissa_bits=7)
        total += jnp.where(lane == place, high, 0.0)
        total += jnp.where(lane == place + shift, value - high, 0.0)
    return total.astype(jnp.bfloat16)


def section_step(
    fresh, cotangent, prev_out, prev_grad, saved_in, route_fwd, route_bwd, router, gate_up, down
):
    section_index = lax.axis_index("pipe")
    sections = lax.axis_size("pipe")
    replicas = lax.axis_size("dp")
    owners = lax.axis_size("expert")
    mine = lax.axis_index("expert")
    inputs_bwd = saved_in[0]
    router_w = router[0]
    gate_up_w = gate_up[0, 0]
    down_w = down[0, 0]
    tokens, width = fresh.shape
    experts = router_w.shape[1]
    hidden_width = down_w.shape[0]

    rows_bwd = gather(inputs_bwd)
    returned = passed_along(prev_grad[0], "pipe", -1)
    arrived = passed_along(prev_out[0], "pipe", 1)
    inverse_bwd = inverse_spread(inputs_bwd)
    unit_bwd = inputs_bwd.astype(jnp.float32) * inverse_bwd
    gates = gate_pair(unit_bwd.astype(jnp.bfloat16), router_w, route_bwd[0])
    upstream = jnp.where(section_index == sections - 1, cotangent, returned)
    side = side_columns(gates, route_bwd[0], inverse_bwd, experts)
    ups = gather(jnp.concatenate([upstream, side], axis=1))

    inputs_fwd = jnp.where(section_index == 0, fresh, arrived)
    inverse_fwd = inverse_spread(inputs_fwd)
    normed_fwd = (inputs_fwd.astype(jnp.float32) * inverse_fwd).astype(jnp.bfloat16)
    gates = gate_pair(normed_fwd, router_w, route_fwd[0])
    side = side_columns(gates, route_fwd[0], inverse_fwd, experts)
    rows_fwd = gather(jnp.concatenate([inputs_fwd, side], axis=1))

    count = owners * tokens
    share = width // replicas
    scalar = mine.astype(jnp.int32).reshape(1)
    router_turned = jnp.pad(router_w.T, ((0, LANES - experts), (0, 0)))
    flops = 2 * count * width * hidden_width
    (projected,) = kernel_call(
        functools.partial(project_kernel, owners),
        (*rows_bwd, gate_up_w),
        [jax.ShapeDtypeStruct((count, 2 * hidden_width), jnp.float32)],
        2 * flops,
    )
    early = owners - 2

    def middle(first, last):
        size = (last - first) * tokens
        return kernel_call(
            functools.partial(middle_kernel, last - first, experts, first * tokens),
            (scalar, projected, down_w, *ups[first:last]),
            [
                jax.ShapeDtypeStruct((size, 2 * hidden_width), jnp.bfloat16),
                jax.ShapeDtypeStruct((size, LANES), jnp.bfloat16),
                jax.ShapeDtypeStruct((2 * hidden_width + ROUTER_ROWS, size), jnp.bfloat16),
                jax.ShapeDtypeStruct((hidden_width, size), jnp.bfloat16),
            ],
            flops * (last - first) // owners,
            [pltpu.VMEM((size, hidden_width), jnp.float32), pltpu.VMEM((size, LANES), jnp.float32)],
            1,
        )

    early_grads, early_steps, early_first, early_second = middle(0, early)
    late_grads, late_steps, late_first, late_second = middle(early, owners)
    place = lax.axis_index("dp").astype(jnp.int32).reshape(1)
    lefts = replicas // 2 + 1
    left_parts, right_parts, router_part = kernel_call(
        functools.partial(weights_kernel, owners),
        (place, early_first, late_first, early_second, late_second, *rows_bwd, *ups),
        [
            jax.ShapeDtypeStruct((lefts, 3 * hidden_width, share), jnp.bfloat16),
            jax.ShapeDtypeStruct((replicas - lefts, 3 * hidden_width, share), jnp.bfloat16),
            jax.ShapeDtypeStruct((replicas * experts, share), jnp.float32),
        ],
        3 * flops,
        (),
        1,
    )

    def block_of(number, wide):
        return jax.ShapeDtypeStruct((number * tokens, wide), jnp.bfloat16)

    wide = width + LANES
    own, near, back, far, far_other, back_other, others = kernel_call(
        functools.partial(rows_kernel, owners),
        (
            scalar,
            early_grads,
            late_grads,
            early_steps,
            late_steps,
            gate_up_w,
            router_turned,
            router_part,
        ),
        [block_of(1, wide)] * 6 + [block_of(2, wide)],
        2 * flops,
        [pltpu.VMEM((count, LANES), jnp.float32)],
        1,
    )
    back_rows = scatter_sum((own, near, back, far), far_other, back_other, others)

    def forward(first, last, outs):
        size = (last - first) * tokens
        return kernel_call(
            functools.partial(forward_kernel, last - first, experts, first),
            (scalar, gate_up_w, down_w, *rows_fwd[first:last]),
            outs,
            3 * flops * (last - first) // owners,
            [
                pltpu.VMEM((size, 2 * hidden_width), jnp.float32),
                pltpu.VMEM((size, LANES), jnp.float32),
                pltpu.VMEM((size, hidden_width), jnp.bfloat16),
            ],
            1,
        )

    own, near, back, back_other, others = forward(
        0, early, [block_of(1, width)] * 4 + [block_of(2, width)]
    )
    far, far_other = forward(early, owners, [block_of(1, width)] * 2)

    def ring_sum(away, terms):
        pairs = [(i, (i + away) % replicas) for i in range(replicas)]
        running = terms[0]
        for hop in range(1, len(terms) + 1):
            if hop > 1:
                term = terms[hop - 1]
                running = (moved.astype(jnp.float32) + term.astype(jnp.float32)).astype(jnp.bfloat16)
            moved = lax.ppermute(running, "dp", pairs)
        return moved.astype(jnp.float32)

    weight_sums = ring_sum(1, [left_parts[i] for i in range(lefts - 1, 0, -1)])
    weight_sums += ring_sum(-1, [right_parts[i] for i in range(replicas - lefts)])
    weight_sums = (weight_sums + left_parts[0].astype(jnp.float32)).astype(jnp.bfloat16)
    normed_grad = back_rows[:, :width]
    inner_mean = jnp.mean(normed_grad * unit_bwd, axis=1, keepdims=True)
    grad_value = upstream.astype(jnp.float32) + (normed_grad - unit_bwd * inner_mean) * inverse_bwd
    input_grad = grad_value.astype(jnp.bfloat16)
    back_fwd = scatter_sum((own, near, back, far), far_other, back_other, others)
    section_out = (inputs_fwd.astype(jnp.float32) + back_fwd).astype(jnp.bfloat16)

    grad_gate_up = weight_sums[: 2 * hidden_width].T
    grad_down = weight_sums[2 * hidden_width :]
    router_sum = back_rows[: replicas * experts, width : width + share // owners]
    half = replicas // 2
    while half:
        pairs = [(i, i ^ half) for i in range(replicas)]
        moved = lax.ppermute(router_sum[half * experts :], "dp", pairs)
        router_sum = router_sum[: half * experts] + moved
        half = half // 2
    grad_router = router_sum.T
    return (
        section_out[None],
        input_grad[None],
        grad_gate_up[None, None],
        grad_down[None, None],
        grad_router[None],
    )


def solution(mesh):
    placed = (
        P(("dp", "expert"), None),
        P(("dp", "expert"), None),
        P("pipe", ("dp", "expert"), None),
        P("pipe", ("dp", "expert"), None),
        P("pipe", ("dp", "expert"), None),
        P("pipe", ("dp", "expert"), None),
        P("pipe", ("dp", "expert"), None),
        P("pipe", None, None),
        P("pipe", "expert", None, None),
        P("pipe", "expert", None, None),
    )
    return jax.shard_map(
        section_step,
        mesh=mesh,
        in_specs=placed,
        out_specs=(
            P("pipe", ("dp", "expert"), None),
            P("pipe", ("dp", "expert"), None),
            P("pipe", "expert", "dp", None),
            P("pipe", "expert", None, "dp"),
            P("pipe", ("dp", "expert"), None),
        ),
        check_vma=False,
    )
```

```python
import functools

import jax
import jax.numpy as jnp
from jax import lax
from jax.experimental import pallas as pl
from jax.experimental.pallas import tpu as pltpu
from jax.sharding import PartitionSpec as P


EPSILON = 1e-05
LANES = 128
ROUTER_ROWS = 16
CHUNK = 512


def passed_along(x, axis, by):
    length = lax.axis_size(axis)
    pairs = [(i, i + by) for i in range(length) if 0 <= i + by < length]
    return lax.ppermute(x, axis, pairs)


def ring_pairs(away):
    chips = lax.axis_size("expert") // 2
    pairs = []
    for chip in range(chips):
        for core in range(2):
            step = away if core == 0 else -away
            pairs.append((2 * chip + core, 2 * ((chip + step) % chips) + core))
    return pairs


def ahead(x):
    return lax.ppermute(x, "expert", ring_pairs(1))


def behind(x):
    return lax.ppermute(x, "expert", ring_pairs(-1))


def swapped(x):
    return lax.ppermute(x, "expert", [(i, i ^ 1) for i in range(lax.axis_size("expert"))])


def gather(block):
    near = ahead(block)
    back = behind(block)
    own_other = swapped(block)
    far = ahead(near)
    near_other = swapped(near)
    back_other = swapped(back)
    far_other = swapped(far)
    return [block, own_other, near, near_other, back, back_other, far, far_other]


def scatter_sum(mine, far_other, back_other, others):
    own, near, back, far = mine
    tokens = own.shape[0]

    def wide(x):
        return x.astype(jnp.float32)

    far_other = swapped(far_other)
    back_other = swapped(back_other)
    others = swapped(others)
    far = (wide(far) + wide(far_other)).astype(jnp.bfloat16)
    passing = behind(far)
    back = (wide(back) + wide(back_other)).astype(jnp.bfloat16)
    from_back = ahead(back)
    near = (wide(near) + wide(others[:tokens]) + wide(passing)).astype(jnp.bfloat16)
    from_near = behind(near)
    return wide(own) + wide(others[tokens:]) + wide(from_back) + wide(from_near)


def contract_cols(first_operand, second_operand):
    return lax.dot_general(
        first_operand, second_operand, (((1,), (1,)), ((), ())), preferred_element_type=jnp.float32
    )


def stacked(blocks, columns):
    return jnp.concatenate([block[:, columns] for block in blocks], axis=0)


def over_chunks(width, chunk, step):
    def body(index, carry):
        step(index, pl.ds(pl.multiple_of(index * chunk, chunk), chunk))
        return carry

    lax.fori_loop(0, width // chunk, body, 0)


def over_rows(count, step):
    def body(index, carry):
        step(pl.ds(pl.multiple_of(index * LANES, LANES), LANES))
        return carry

    lax.fori_loop(0, count // LANES, body, 0)


def read_side(columns, experts, mine):
    table = columns[:, :experts] + columns[:, experts : 2 * experts]
    lane = lax.broadcasted_iota(jnp.int32, table.shape, 1)
    weight = jnp.sum(jnp.where(lane == mine, table, 0.0), axis=1, keepdims=True)
    inverse = columns[:, 2 * experts : 2 * experts + 1] + columns[:, 2 * experts + 1 : 2 * experts + 2]
    return (table, lane, weight, inverse)


def project_kernel(owners, *refs):
    blocks, gate_up, projected = refs[:owners], refs[owners], refs[owners + 1]
    projected[...] = jnp.zeros_like(projected)

    def step(index, columns):
        projected[...] += jnp.dot(
            stacked(blocks, columns), gate_up[columns, :], preferred_element_type=jnp.float32
        )

    over_chunks(gate_up.shape[0], CHUNK, step)


def middle_kernel(owners, experts, first_row, *refs):
    mine_ref, projected_ref, down = refs[:3]
    blocks = refs[3 : 3 + owners]
    grads, steps, first_turned, second_turned, bare, side = refs[3 + owners :]
    hidden_width, width = down.shape
    count = grads.shape[0]
    mine = mine_ref[0]
    bare[...] = jnp.zeros_like(bare)
    side[...] = stacked(blocks, slice(width, width + LANES)).astype(jnp.float32)

    def step(index, columns):
        bare[...] += contract_cols(stacked(blocks, columns), down[:, columns])

    over_chunks(width, CHUNK, step)

    def finish(rows):
        table, lane, weight, inverse = read_side(side[rows, :], experts, mine)
        projected = projected_ref[pl.ds(rows.start + first_row, LANES), :] * inverse
        pre_gate = projected[:, :hidden_width]
        pre_up = projected[:, hidden_width:]
        sigmoid_gate = jax.nn.sigmoid(pre_gate)
        active = pre_gate * sigmoid_gate
        hidden = active * pre_up
        bare_grad = bare[rows, :]
        gate_grad = jnp.sum(hidden * bare_grad, axis=1, keepdims=True)
        hidden_grad = bare_grad * weight
        grad_g = hidden_grad * pre_up * sigmoid_gate * (1.0 + pre_gate * (1.0 - sigmoid_gate))
        grad_u = hidden_grad * active
        other = jnp.sum(table, axis=1, keepdims=True) - weight
        sign = jnp.where(lane == mine, 1.0, jnp.where(table > 0.0, -1.0, 0.0))
        logit_part = weight * other * gate_grad * sign
        logit_part = jnp.concatenate(
            [logit_part, jnp.zeros((LANES, LANES - experts), jnp.float32)], axis=1
        )
        grads[rows, :hidden_width] = grad_g.astype(jnp.bfloat16)
        grads[rows, hidden_width:] = grad_u.astype(jnp.bfloat16)
        steps[rows, :] = logit_part.astype(jnp.bfloat16)
        first_turned[:hidden_width, rows] = (grad_g * inverse).T.astype(jnp.bfloat16)
        first_turned[hidden_width : 2 * hidden_width, rows] = (grad_u * inverse).T.astype(jnp.bfloat16)
        first_turned[2 * hidden_width :, rows] = (logit_part * inverse).T[:ROUTER_ROWS].astype(
            jnp.bfloat16
        )
        second_turned[:, rows] = (hidden * weight).T.astype(jnp.bfloat16)

    over_rows(count, finish)


def weights_kernel(owners, *refs):
    replica_ref, turned, refs = refs[0], refs[1:5], refs[5:]
    rows, ups = refs[:owners], refs[owners : 2 * owners]
    left_out, right_out, router_out = refs[2 * owners :]
    _, share = left_out.shape[1:]
    replicas = left_out.shape[0] + right_out.shape[0]
    lefts = left_out.shape[0]
    middle = turned[0].shape[0] - ROUTER_ROWS
    experts = router_out.shape[0] // replicas
    replica = replica_ref[0]

    def chunk(shift, carry):
        target = (replica + shift) % replicas

        columns = pl.ds(pl.multiple_of(target * share, share), share)
        first = jnp.dot(
            jnp.concatenate([turned[0][...], turned[1][...]], axis=1),
            stacked(rows, columns),
            preferred_element_type=jnp.float32,
        )
        second = jnp.dot(
            jnp.concatenate([turned[2][...], turned[3][...]], axis=1),
            stacked(ups, columns),
            preferred_element_type=jnp.float32,
        )

        def put(out, slot):
            out[slot, :middle, :] = first[:middle].astype(jnp.bfloat16)
            out[slot, middle:, :] = second.astype(jnp.bfloat16)

        @pl.when(shift < lefts)
        def _():
            put(left_out, shift)

        @pl.when(shift >= lefts)
        def _():
            put(right_out, shift - lefts)

        line = pl.ds(pl.multiple_of((target ^ replica) * experts, experts), experts)
        router_out[line, :] = first[middle : middle + experts]
        return carry

    lax.fori_loop(0, replicas, chunk, 0)


def store_rows(result, columns, mine, far_other, back_other, others, first, tokens):
    places = [(mine[0], 0), (others, 1), (mine[1], 0), (others, 0), (mine[2], 0), (back_other, 0)]
    places = [*places, (mine[3], 0), (far_other, 0)]
    for index in range(result.shape[0] // tokens):
        out, slot = places[first + index]
        rows = slice(slot * tokens, (slot + 1) * tokens)
        out[rows, columns] = result[index * tokens : (index + 1) * tokens].astype(jnp.bfloat16)


def rows_kernel(owners, *refs):
    mine_ref, early_grads, late_grads, early_steps, late_steps, gate_up, router_turned, router_part = refs[:8]
    own, near, back, far, far_other, back_other, others, side = refs[8:]
    mine_refs = (own, near, back, far)
    tokens = own.shape[0]
    width = gate_up.shape[0]
    lines, share = router_part.shape
    piece = share // owners

    def step(index, columns):
        result = contract_cols(
            jnp.concatenate([early_grads[...], late_grads[...]], axis=0), gate_up[columns, :]
        )
        result += jnp.dot(
            jnp.concatenate([early_steps[...], late_steps[...]], axis=0),
            router_turned[:, columns],
            preferred_element_type=jnp.float32,
        )
        store_rows(result, columns, mine_refs, far_other, back_other, others, 0, tokens)

    over_chunks(width, CHUNK, step)
    me = mine_ref[0]
    chips = owners // 2
    chip, core = me // 2, me % 2
    way = 1 - 2 * core
    part = router_part[...].astype(jnp.bfloat16)
    row = lax.broadcasted_iota(jnp.int32, (share, LANES), 0)
    lane = lax.broadcasted_iota(jnp.int32, (share, LANES), 1)
    side[...] = jnp.zeros_like(side)

    def block(index, carry):
        pair, crossed = index // 2, index % 2
        back_way = way * (1 - 2 * crossed)
        move = jnp.where(pair == 1, -back_way, jnp.where(pair == 2, back_way, jnp.where(pair == 3, 2, 0)))
        owner = 2 * ((chip + move + chips) % chips) + jnp.where(crossed == 1, 1 - core, core)
        hot = jnp.where((row == owner * piece + lane) & (lane < piece), 1.0, 0.0).astype(jnp.bfloat16)
        block_rows = pl.ds(pl.multiple_of(index * tokens, tokens), lines)
        side[block_rows, :] = jnp.dot(part, hot, preferred_element_type=jnp.float32)
        return carry

    lax.fori_loop(0, owners, block, 0)
    store_rows(
        side[...],
        slice(width, width + LANES),
        mine_refs,
        far_other,
        back_other,
        others,
        0,
        tokens,
    )


def forward_kernel(owners, experts, first, *refs):
    mine_ref, gate_up, down = refs[:3]
    blocks, outs = refs[3 : 3 + owners], refs[3 + owners : -3]
    projected_ref, side, hidden_ref = refs[-3:]
    hidden_width, width = down.shape
    tokens = blocks[0].shape[0]
    projected_ref[...] = jnp.zeros_like(projected_ref)

    def project(index, columns):
        projected_ref[...] += jnp.dot(
            stacked(blocks, columns), gate_up[columns, :], preferred_element_type=jnp.float32
        )

    over_chunks(width, CHUNK, project)
    side[...] = stacked(blocks, slice(width, width + LANES)).astype(jnp.float32)

    def finish(rows):
        _, _, weight, inverse = read_side(side[rows, :], experts, mine_ref[0])
        projected = projected_ref[rows, :] * inverse
        pre_gate = projected[:, :hidden_width]
        pre_up = projected[:, hidden_width:]
        hidden_ref[rows, :] = (pre_gate * jax.nn.sigmoid(pre_gate) * pre_up * weight).astype(jnp.bfloat16)

    over_rows(side.shape[0], finish)
    if first:
        mine, far_other, back_other, others = (None, None, None, outs[0]), outs[1], None, None
    else:
        mine, far_other, back_other, others = (*outs[:3], None), None, outs[3], outs[4]

    def step(index, columns):
        result = jnp.dot(hidden_ref[...], down[:, columns], preferred_element_type=jnp.float32)
        store_rows(result, columns, mine, far_other, back_other, others, first, tokens)

    over_chunks(width, CHUNK, step)


def kernel_call(kernel, operands, outs, flops, scratch=(), scalars=0):
    whole = pl.BlockSpec(memory_space=pltpu.VMEM)
    scalar = pl.BlockSpec(memory_space=pltpu.SMEM)
    return pl.pallas_call(
        kernel,
        out_shape=outs,
        in_specs=[scalar] * scalars + [whole] * (len(operands) - scalars),
        out_specs=[whole] * len(outs),
        scratch_shapes=list(scratch),
        compiler_params=pltpu.CompilerParams(vmem_limit_bytes=12 << 20),
        cost_estimate=pl.CostEstimate(flops=flops, bytes_accessed=10_000_000, transcendentals=0),
    )(*operands)


def inverse_spread(values):
    values = values.astype(jnp.float32)
    return lax.rsqrt(jnp.mean(values * values, axis=-1, keepdims=True) + EPSILON)


def gate_pair(normed, router_w, routes):
    experts = router_w.shape[1]
    logits = jnp.dot(normed, router_w, preferred_element_type=jnp.float32)
    onehot = (routes[:, :, None] == jnp.arange(experts, dtype=jnp.int32)[None, None, :]).astype(
        jnp.float32
    )
    chosen = jnp.sum(onehot * logits[:, None, :], axis=2)
    return (
        jax.nn.sigmoid(chosen[:, 0:1] - chosen[:, 1:2]),
        jax.nn.sigmoid(chosen[:, 1:2] - chosen[:, 0:1]),
    )


def side_columns(gates, routes, inverse, experts):
    lane = jnp.arange(LANES, dtype=jnp.int32)[None, :]
    places = (routes[:, 0:1], routes[:, 1:2], jnp.full_like(routes[:, 0:1], 2 * experts))
    low_shift = (experts, experts, 1)
    total = jnp.zeros((routes.shape[0], LANES), jnp.float32)
    for value, place, shift in zip((*gates, inverse), places, low_shift):
        high = lax.reduce_precision(value, exponent_bits=8, mantissa_bits=7)
        total += jnp.where(lane == place, high, 0.0)
        total += jnp.where(lane == place + shift, value - high, 0.0)
    return total.astype(jnp.bfloat16)


def section_step(
    fresh, cotangent, prev_out, prev_grad, saved_in, route_fwd, route_bwd, router, gate_up, down
):
    section_index = lax.axis_index("pipe")
    sections = lax.axis_size("pipe")
    replicas = lax.axis_size("dp")
    owners = lax.axis_size("expert")
    mine = lax.axis_index("expert")
    inputs_bwd = saved_in[0]
    router_w = router[0]
    gate_up_w = gate_up[0, 0]
    down_w = down[0, 0]
    tokens, width = fresh.shape
    experts = router_w.shape[1]
    hidden_width = down_w.shape[0]

    rows_bwd = gather(inputs_bwd)
    returned = passed_along(prev_grad[0], "pipe", -1)
    arrived = passed_along(prev_out[0], "pipe", 1)
    inverse_bwd = inverse_spread(inputs_bwd)
    unit_bwd = inputs_bwd.astype(jnp.float32) * inverse_bwd
    gates = gate_pair(unit_bwd.astype(jnp.bfloat16), router_w, route_bwd[0])
    upstream = jnp.where(section_index == sections - 1, cotangent, returned)
    side = side_columns(gates, route_bwd[0], inverse_bwd, experts)
    ups = gather(jnp.concatenate([upstream, side], axis=1))

    inputs_fwd = jnp.where(section_index == 0, fresh, arrived)
    inverse_fwd = inverse_spread(inputs_fwd)
    normed_fwd = (inputs_fwd.astype(jnp.float32) * inverse_fwd).astype(jnp.bfloat16)
    gates = gate_pair(normed_fwd, router_w, route_fwd[0])
    side = side_columns(gates, route_fwd[0], inverse_fwd, experts)
    rows_fwd = gather(jnp.concatenate([inputs_fwd, side], axis=1))

    count = owners * tokens
    share = width // replicas
    scalar = mine.astype(jnp.int32).reshape(1)
    router_turned = jnp.pad(router_w.T, ((0, LANES - experts), (0, 0)))
    flops = 2 * count * width * hidden_width
    (projected,) = kernel_call(
        functools.partial(project_kernel, owners),
        (*rows_bwd, gate_up_w),
        [jax.ShapeDtypeStruct((count, 2 * hidden_width), jnp.float32)],
        2 * flops,
    )
    early = owners - 2

    def middle(first, last):
        size = (last - first) * tokens
        return kernel_call(
            functools.partial(middle_kernel, last - first, experts, first * tokens),
            (scalar, projected, down_w, *ups[first:last]),
            [
                jax.ShapeDtypeStruct((size, 2 * hidden_width), jnp.bfloat16),
                jax.ShapeDtypeStruct((size, LANES), jnp.bfloat16),
                jax.ShapeDtypeStruct((2 * hidden_width + ROUTER_ROWS, size), jnp.bfloat16),
                jax.ShapeDtypeStruct((hidden_width, size), jnp.bfloat16),
            ],
            flops * (last - first) // owners,
            [pltpu.VMEM((size, hidden_width), jnp.float32), pltpu.VMEM((size, LANES), jnp.float32)],
            1,
        )

    early_grads, early_steps, early_first, early_second = middle(0, early)
    late_grads, late_steps, late_first, late_second = middle(early, owners)
    place = lax.axis_index("dp").astype(jnp.int32).reshape(1)
    lefts = replicas // 2 + 1
    left_parts, right_parts, router_part = kernel_call(
        functools.partial(weights_kernel, owners),
        (place, early_first, late_first, early_second, late_second, *rows_bwd, *ups),
        [
            jax.ShapeDtypeStruct((lefts, 3 * hidden_width, share), jnp.bfloat16),
            jax.ShapeDtypeStruct((replicas - lefts, 3 * hidden_width, share), jnp.bfloat16),
            jax.ShapeDtypeStruct((replicas * experts, share), jnp.float32),
        ],
        3 * flops,
        (),
        1,
    )

    def block_of(number, wide):
        return jax.ShapeDtypeStruct((number * tokens, wide), jnp.bfloat16)

    wide = width + LANES
    own, near, back, far, far_other, back_other, others = kernel_call(
        functools.partial(rows_kernel, owners),
        (
            scalar,
            early_grads,
            late_grads,
            early_steps,
            late_steps,
            gate_up_w,
            router_turned,
            router_part,
        ),
        [block_of(1, wide)] * 6 + [block_of(2, wide)],
        2 * flops,
        [pltpu.VMEM((count, LANES), jnp.float32)],
        1,
    )
    back_rows = scatter_sum((own, near, back, far), far_other, back_other, others)

    def forward(first, last, outs):
        size = (last - first) * tokens
        return kernel_call(
            functools.partial(forward_kernel, last - first, experts, first),
            (scalar, gate_up_w, down_w, *rows_fwd[first:last]),
            outs,
            3 * flops * (last - first) // owners,
            [
                pltpu.VMEM((size, 2 * hidden_width), jnp.float32),
                pltpu.VMEM((size, LANES), jnp.float32),
                pltpu.VMEM((size, hidden_width), jnp.bfloat16),
            ],
            1,
        )

    own, near, back, back_other, others = forward(
        0, early, [block_of(1, width)] * 4 + [block_of(2, width)]
    )
    far, far_other = forward(early, owners, [block_of(1, width)] * 2)

    half = 3 * hidden_width // 2

    def ring_sum(away, start, terms):
        pairs = [(i, (i + away) % replicas) for i in range(replicas)]
        running = start
        for hop in range(1, len(terms) + 2):
            if hop > 1:
                term = terms[hop - 2].astype(jnp.float32)
                added = moved.astype(jnp.float32)
                if hop == 2:
                    kept = (term[half:], term[:half])[away < 0]
                    summed = (term[:half], term[half:])[away < 0] + added
                    running = jnp.concatenate([summed, kept] if away > 0 else [kept, summed], axis=0)
                else:
                    running = term + added
                running = running.astype(jnp.bfloat16)
            moved = lax.ppermute(running, "dp", pairs)
        return moved.astype(jnp.float32)

    farthest = left_parts[lefts - 1]
    weight_sums = ring_sum(1, farthest[:half], [left_parts[i] for i in range(lefts - 2, 0, -1)])
    weight_sums += ring_sum(-1, farthest[half:], [right_parts[i] for i in range(replicas - lefts)])
    weight_sums = (weight_sums + left_parts[0].astype(jnp.float32)).astype(jnp.bfloat16)
    normed_grad = back_rows[:, :width]
    inner_mean = jnp.mean(normed_grad * unit_bwd, axis=1, keepdims=True)
    grad_value = upstream.astype(jnp.float32) + (normed_grad - unit_bwd * inner_mean) * inverse_bwd
    input_grad = grad_value.astype(jnp.bfloat16)
    back_fwd = scatter_sum((own, near, back, far), far_other, back_other, others)
    section_out = (inputs_fwd.astype(jnp.float32) + back_fwd).astype(jnp.bfloat16)

    grad_gate_up = weight_sums[: 2 * hidden_width].T
    grad_down = weight_sums[2 * hidden_width :]
    router_sum = back_rows[: replicas * experts, width : width + share // owners]
    half = replicas // 2
    while half:
        pairs = [(i, i ^ half) for i in range(replicas)]
        moved = lax.ppermute(router_sum[half * experts :], "dp", pairs)
        router_sum = router_sum[: half * experts] + moved
        half = half // 2
    grad_router = router_sum.T
    return (
        section_out[None],
        input_grad[None],
        grad_gate_up[None, None],
        grad_down[None, None],
        grad_router[None],
    )


def solution(mesh):
    placed = (
        P(("dp", "expert"), None),
        P(("dp", "expert"), None),
        P("pipe", ("dp", "expert"), None),
        P("pipe", ("dp", "expert"), None),
        P("pipe", ("dp", "expert"), None),
        P("pipe", ("dp", "expert"), None),
        P("pipe", ("dp", "expert"), None),
        P("pipe", None, None),
        P("pipe", "expert", None, None),
        P("pipe", "expert", None, None),
    )
    return jax.shard_map(
        section_step,
        mesh=mesh,
        in_specs=placed,
        out_specs=(
            P("pipe", ("dp", "expert"), None),
            P("pipe", ("dp", "expert"), None),
            P("pipe", "expert", "dp", None),
            P("pipe", "expert", None, "dp"),
            P("pipe", ("dp", "expert"), None),
        ),
        check_vma=False,
    )
```

```python
import functools

import jax
import jax.numpy as jnp
from jax import lax
from jax.experimental import pallas as pl
from jax.experimental.pallas import tpu as pltpu
from jax.sharding import PartitionSpec as P


EPSILON = 1e-05
LANES = 128
ROUTER_ROWS = 16
CHUNK = 512


def passed_along(x, axis, by):
    length = lax.axis_size(axis)
    pairs = [(i, i + by) for i in range(length) if 0 <= i + by < length]
    return lax.ppermute(x, axis, pairs)


def ring_pairs(away):
    chips = lax.axis_size("expert") // 2
    pairs = []
    for chip in range(chips):
        for core in range(2):
            step = away if core == 0 else -away
            pairs.append((2 * chip + core, 2 * ((chip + step) % chips) + core))
    return pairs


def ahead(x):
    return lax.ppermute(x, "expert", ring_pairs(1))


def behind(x):
    return lax.ppermute(x, "expert", ring_pairs(-1))


def swapped(x):
    return lax.ppermute(x, "expert", [(i, i ^ 1) for i in range(lax.axis_size("expert"))])


def gather(block):
    near = ahead(block)
    back = behind(block)
    own_other = swapped(block)
    far = ahead(near)
    near_other = swapped(near)
    back_other = swapped(back)
    far_other = swapped(far)
    return [block, own_other, near, near_other, back, back_other, far, far_other]


def scatter_sum(mine, far_other, back_other, others, base=None):
    own, near, back, far = mine
    tokens = own.shape[0]

    def wide(x):
        return x.astype(jnp.float32)

    far_other = swapped(far_other)
    back_other = swapped(back_other)
    others = swapped(others)
    far = (wide(far) + wide(far_other)).astype(jnp.bfloat16)
    passing = behind(far)
    back = (wide(back) + wide(back_other)).astype(jnp.bfloat16)
    from_back = ahead(back)
    near = (wide(near) + wide(others[:tokens]) + wide(passing)).astype(jnp.bfloat16)
    from_near = behind(near)
    total = wide(own) + wide(others[tokens:]) + wide(from_back)
    if base is not None:
        total = lax.optimization_barrier(total + wide(base))
    return total + wide(from_near)


def contract_cols(first_operand, second_operand):
    return lax.dot_general(
        first_operand, second_operand, (((1,), (1,)), ((), ())), preferred_element_type=jnp.float32
    )


def stacked(blocks, columns):
    return jnp.concatenate([block[:, columns] for block in blocks], axis=0)


def over_chunks(width, chunk, step):
    def body(index, carry):
        step(index, pl.ds(pl.multiple_of(index * chunk, chunk), chunk))
        return carry

    lax.fori_loop(0, width // chunk, body, 0)


def over_rows(count, step):
    def body(index, carry):
        step(pl.ds(pl.multiple_of(index * LANES, LANES), LANES))
        return carry

    lax.fori_loop(0, count // LANES, body, 0)


def read_side(columns, experts, mine):
    table = columns[:, :experts] + columns[:, experts : 2 * experts]
    lane = lax.broadcasted_iota(jnp.int32, table.shape, 1)
    weight = jnp.sum(jnp.where(lane == mine, table, 0.0), axis=1, keepdims=True)
    inverse = columns[:, 2 * experts : 2 * experts + 1] + columns[:, 2 * experts + 1 : 2 * experts + 2]
    return (table, lane, weight, inverse)


def project_kernel(owners, *refs):
    blocks, gate_up, projected = refs[:owners], refs[owners], refs[owners + 1]
    projected[...] = jnp.zeros_like(projected)

    def step(index, columns):
        projected[...] += jnp.dot(
            stacked(blocks, columns), gate_up[columns, :], preferred_element_type=jnp.float32
        )

    over_chunks(gate_up.shape[0], CHUNK, step)


def middle_kernel(owners, experts, first_row, *refs):
    mine_ref, projected_ref, down = refs[:3]
    blocks = refs[3 : 3 + owners]
    grads, steps, first_turned, second_turned, bare, side = refs[3 + owners :]
    hidden_width, width = down.shape
    count = grads.shape[0]
    mine = mine_ref[0]
    bare[...] = jnp.zeros_like(bare)
    side[...] = stacked(blocks, slice(width, width + LANES)).astype(jnp.float32)

    def step(index, columns):
        bare[...] += contract_cols(stacked(blocks, columns), down[:, columns])

    over_chunks(width, CHUNK, step)

    def finish(rows):
        table, lane, weight, inverse = read_side(side[rows, :], experts, mine)
        projected = projected_ref[pl.ds(rows.start + first_row, LANES), :] * inverse
        pre_gate = projected[:, :hidden_width]
        pre_up = projected[:, hidden_width:]
        sigmoid_gate = jax.nn.sigmoid(pre_gate)
        active = pre_gate * sigmoid_gate
        hidden = active * pre_up
        bare_grad = bare[rows, :]
        gate_grad = jnp.sum(hidden * bare_grad, axis=1, keepdims=True)
        hidden_grad = bare_grad * weight
        grad_g = hidden_grad * pre_up * sigmoid_gate * (1.0 + pre_gate * (1.0 - sigmoid_gate))
        grad_u = hidden_grad * active
        other = jnp.sum(table, axis=1, keepdims=True) - weight
        sign = jnp.where(lane == mine, 1.0, jnp.where(table > 0.0, -1.0, 0.0))
        logit_part = weight * other * gate_grad * sign
        logit_part = jnp.concatenate(
            [logit_part, jnp.zeros((LANES, LANES - experts), jnp.float32)], axis=1
        )
        grads[rows, :hidden_width] = grad_g.astype(jnp.bfloat16)
        grads[rows, hidden_width:] = grad_u.astype(jnp.bfloat16)
        steps[rows, :] = logit_part.astype(jnp.bfloat16)
        first_turned[:hidden_width, rows] = (grad_g * inverse).T.astype(jnp.bfloat16)
        first_turned[hidden_width : 2 * hidden_width, rows] = (grad_u * inverse).T.astype(jnp.bfloat16)
        first_turned[2 * hidden_width :, rows] = (logit_part * inverse).T[:ROUTER_ROWS].astype(
            jnp.bfloat16
        )
        second_turned[:, rows] = (hidden * weight).T.astype(jnp.bfloat16)

    over_rows(count, finish)


def weights_kernel(owners, *refs):
    replica_ref, turned, refs = refs[0], refs[1:5], refs[5:]
    rows, ups = refs[:owners], refs[owners : 2 * owners]
    left_out, right_out, router_out = refs[2 * owners :]
    _, share = left_out.shape[1:]
    replicas = left_out.shape[0] + right_out.shape[0]
    lefts = left_out.shape[0]
    middle = turned[0].shape[0] - ROUTER_ROWS
    experts = router_out.shape[0] // replicas
    replica = replica_ref[0]

    def chunk(shift, carry):
        target = (replica + shift) % replicas

        columns = pl.ds(pl.multiple_of(target * share, share), share)
        first = jnp.dot(
            jnp.concatenate([turned[0][...], turned[1][...]], axis=1),
            stacked(rows, columns),
            preferred_element_type=jnp.float32,
        )
        second = jnp.dot(
            jnp.concatenate([turned[2][...], turned[3][...]], axis=1),
            stacked(ups, columns),
            preferred_element_type=jnp.float32,
        )

        def put(out, slot):
            out[slot, :middle, :] = first[:middle].astype(jnp.bfloat16)
            out[slot, middle:, :] = second.astype(jnp.bfloat16)

        @pl.when(shift < lefts)
        def _():
            put(left_out, shift)

        @pl.when(shift >= lefts)
        def _():
            put(right_out, shift - lefts)

        line = pl.ds(pl.multiple_of(target * experts, experts), experts)
        router_out[line, :] = first[middle : middle + experts]
        return carry

    lax.fori_loop(0, replicas, chunk, 0)


def store_rows(result, columns, mine, far_other, back_other, others, first, tokens):
    places = [(mine[0], 0), (others, 1), (mine[1], 0), (others, 0), (mine[2], 0), (back_other, 0)]
    places = [*places, (mine[3], 0), (far_other, 0)]
    for index in range(result.shape[0] // tokens):
        out, slot = places[first + index]
        rows = slice(slot * tokens, (slot + 1) * tokens)
        out[rows, columns] = result[index * tokens : (index + 1) * tokens].astype(jnp.bfloat16)


def rows_kernel(owners, *refs):
    mine_ref, early_grads, late_grads, early_steps, late_steps, gate_up, router_turned, router_part = refs[:8]
    own, near, back, far, far_other, back_other, others, side = refs[8:]
    mine_refs = (own, near, back, far)
    tokens = own.shape[0]
    width = gate_up.shape[0]
    lines, share = router_part.shape
    piece = share // owners

    def step(index, columns):
        result = contract_cols(
            jnp.concatenate([early_grads[...], late_grads[...]], axis=0), gate_up[columns, :]
        )
        result += jnp.dot(
            jnp.concatenate([early_steps[...], late_steps[...]], axis=0),
            router_turned[:, columns],
            preferred_element_type=jnp.float32,
        )
        store_rows(result, columns, mine_refs, far_other, back_other, others, 0, tokens)

    over_chunks(width, CHUNK, step)
    me = mine_ref[0]
    chips = owners // 2
    chip, core = me // 2, me % 2
    way = 1 - 2 * core
    part = router_part[...].astype(jnp.bfloat16)
    row = lax.broadcasted_iota(jnp.int32, (share, LANES), 0)
    lane = lax.broadcasted_iota(jnp.int32, (share, LANES), 1)
    side[...] = jnp.zeros_like(side)

    def block(index, carry):
        pair, crossed = index // 2, index % 2
        back_way = way * (1 - 2 * crossed)
        move = jnp.where(pair == 1, -back_way, jnp.where(pair == 2, back_way, jnp.where(pair == 3, 2, 0)))
        owner = 2 * ((chip + move + chips) % chips) + jnp.where(crossed == 1, 1 - core, core)
        hot = jnp.where((row == owner * piece + lane) & (lane < piece), 1.0, 0.0).astype(jnp.bfloat16)
        block_rows = pl.ds(pl.multiple_of(index * tokens, tokens), lines)
        side[block_rows, :] = jnp.dot(part, hot, preferred_element_type=jnp.float32)
        return carry

    lax.fori_loop(0, owners, block, 0)
    store_rows(
        side[...],
        slice(width, width + LANES),
        mine_refs,
        far_other,
        back_other,
        others,
        0,
        tokens,
    )


def forward_kernel(owners, experts, first, *refs):
    mine_ref, gate_up, down = refs[:3]
    blocks, outs = refs[3 : 3 + owners], refs[3 + owners : -3]
    projected_ref, side, hidden_ref = refs[-3:]
    hidden_width, width = down.shape
    tokens = blocks[0].shape[0]
    projected_ref[...] = jnp.zeros_like(projected_ref)

    def project(index, columns):
        projected_ref[...] += jnp.dot(
            stacked(blocks, columns), gate_up[columns, :], preferred_element_type=jnp.float32
        )

    over_chunks(width, CHUNK, project)
    side[...] = stacked(blocks, slice(width, width + LANES)).astype(jnp.float32)

    def finish(rows):
        _, _, weight, inverse = read_side(side[rows, :], experts, mine_ref[0])
        projected = projected_ref[rows, :] * inverse
        pre_gate = projected[:, :hidden_width]
        pre_up = projected[:, hidden_width:]
        hidden_ref[rows, :] = (pre_gate * jax.nn.sigmoid(pre_gate) * pre_up * weight).astype(jnp.bfloat16)

    over_rows(side.shape[0], finish)
    if first:
        mine, far_other, back_other, others = (None, None, None, outs[0]), outs[1], None, None
    else:
        mine, far_other, back_other, others = (*outs[:3], None), None, outs[3], outs[4]

    def step(index, columns):
        result = jnp.dot(hidden_ref[...], down[:, columns], preferred_element_type=jnp.float32)
        store_rows(result, columns, mine, far_other, back_other, others, first, tokens)

    over_chunks(width, CHUNK, step)


def kernel_call(kernel, operands, outs, flops, scratch=(), scalars=0):
    whole = pl.BlockSpec(memory_space=pltpu.VMEM)
    scalar = pl.BlockSpec(memory_space=pltpu.SMEM)
    return pl.pallas_call(
        kernel,
        out_shape=outs,
        in_specs=[scalar] * scalars + [whole] * (len(operands) - scalars),
        out_specs=[whole] * len(outs),
        scratch_shapes=list(scratch),
        compiler_params=pltpu.CompilerParams(vmem_limit_bytes=12 << 20),
        cost_estimate=pl.CostEstimate(flops=flops, bytes_accessed=10_000_000, transcendentals=0),
    )(*operands)


def inverse_spread(values):
    values = values.astype(jnp.float32)
    return lax.rsqrt(jnp.mean(values * values, axis=-1, keepdims=True) + EPSILON)


def gate_pair(normed, router_w, routes):
    experts = router_w.shape[1]
    logits = jnp.dot(normed, router_w, preferred_element_type=jnp.float32)
    onehot = (routes[:, :, None] == jnp.arange(experts, dtype=jnp.int32)[None, None, :]).astype(
        jnp.float32
    )
    chosen = jnp.sum(onehot * logits[:, None, :], axis=2)
    return (
        jax.nn.sigmoid(chosen[:, 0:1] - chosen[:, 1:2]),
        jax.nn.sigmoid(chosen[:, 1:2] - chosen[:, 0:1]),
    )


def side_columns(gates, routes, inverse, experts):
    lane = jnp.arange(LANES, dtype=jnp.int32)[None, :]
    places = (routes[:, 0:1], routes[:, 1:2], jnp.full_like(routes[:, 0:1], 2 * experts))
    low_shift = (experts, experts, 1)
    total = jnp.zeros((routes.shape[0], LANES), jnp.float32)
    for value, place, shift in zip((*gates, inverse), places, low_shift):
        high = lax.reduce_precision(value, exponent_bits=8, mantissa_bits=7)
        total += jnp.where(lane == place, high, 0.0)
        total += jnp.where(lane == place + shift, value - high, 0.0)
    return total.astype(jnp.bfloat16)


def section_step(
    fresh, cotangent, prev_out, prev_grad, saved_in, route_fwd, route_bwd, router, gate_up, down
):
    section_index = lax.axis_index("pipe")
    sections = lax.axis_size("pipe")
    replicas = lax.axis_size("dp")
    owners = lax.axis_size("expert")
    mine = lax.axis_index("expert")
    inputs_bwd = saved_in[0]
    router_w = router[0]
    gate_up_w = gate_up[0, 0]
    down_w = down[0, 0]
    tokens, width = fresh.shape
    experts = router_w.shape[1]
    hidden_width = down_w.shape[0]

    rows_bwd = gather(inputs_bwd)
    returned = passed_along(prev_grad[0], "pipe", -1)
    arrived = passed_along(prev_out[0], "pipe", 1)
    inverse_bwd = inverse_spread(inputs_bwd)
    unit_bwd = inputs_bwd.astype(jnp.float32) * inverse_bwd
    gates = gate_pair(unit_bwd.astype(jnp.bfloat16), router_w, route_bwd[0])
    upstream = jnp.where(section_index == sections - 1, cotangent, returned)
    side = side_columns(gates, route_bwd[0], inverse_bwd, experts)
    ups = gather(jnp.concatenate([upstream, side], axis=1))

    inputs_fwd = jnp.where(section_index == 0, fresh, arrived)
    inverse_fwd = inverse_spread(inputs_fwd)
    normed_fwd = (inputs_fwd.astype(jnp.float32) * inverse_fwd).astype(jnp.bfloat16)
    gates = gate_pair(normed_fwd, router_w, route_fwd[0])
    side = side_columns(gates, route_fwd[0], inverse_fwd, experts)
    rows_fwd = gather(jnp.concatenate([inputs_fwd, side], axis=1))

    count = owners * tokens
    share = width // replicas
    scalar = mine.astype(jnp.int32).reshape(1)
    router_turned = jnp.pad(router_w.T, ((0, LANES - experts), (0, 0)))
    flops = 2 * count * width * hidden_width
    (projected,) = kernel_call(
        functools.partial(project_kernel, owners),
        (*rows_bwd, gate_up_w),
        [jax.ShapeDtypeStruct((count, 2 * hidden_width), jnp.float32)],
        2 * flops,
    )
    early = owners - 2

    def middle(first, last):
        size = (last - first) * tokens
        return kernel_call(
            functools.partial(middle_kernel, last - first, experts, first * tokens),
            (scalar, projected, down_w, *ups[first:last]),
            [
                jax.ShapeDtypeStruct((size, 2 * hidden_width), jnp.bfloat16),
                jax.ShapeDtypeStruct((size, LANES), jnp.bfloat16),
                jax.ShapeDtypeStruct((2 * hidden_width + ROUTER_ROWS, size), jnp.bfloat16),
                jax.ShapeDtypeStruct((hidden_width, size), jnp.bfloat16),
            ],
            flops * (last - first) // owners,
            [pltpu.VMEM((size, hidden_width), jnp.float32), pltpu.VMEM((size, LANES), jnp.float32)],
            1,
        )

    early_grads, early_steps, early_first, early_second = middle(0, early)
    late_grads, late_steps, late_first, late_second = middle(early, owners)
    place = lax.axis_index("dp").astype(jnp.int32).reshape(1)
    lefts = replicas // 2 + 1
    left_parts, right_parts, router_part = kernel_call(
        functools.partial(weights_kernel, owners),
        (place, early_first, late_first, early_second, late_second, *rows_bwd, *ups),
        [
            jax.ShapeDtypeStruct((lefts, 3 * hidden_width, share), jnp.bfloat16),
            jax.ShapeDtypeStruct((replicas - lefts, 3 * hidden_width, share), jnp.bfloat16),
            jax.ShapeDtypeStruct((replicas * experts, share), jnp.float32),
        ],
        3 * flops,
        (),
        1,
    )

    def block_of(number, wide):
        return jax.ShapeDtypeStruct((number * tokens, wide), jnp.bfloat16)

    wide = width + LANES
    own, near, back, far, far_other, back_other, others = kernel_call(
        functools.partial(rows_kernel, owners),
        (
            scalar,
            early_grads,
            late_grads,
            early_steps,
            late_steps,
            gate_up_w,
            router_turned,
            router_part,
        ),
        [block_of(1, wide)] * 6 + [block_of(2, wide)],
        2 * flops,
        [pltpu.VMEM((count, LANES), jnp.float32)],
        1,
    )
    back_rows = scatter_sum((own, near, back, far), far_other, back_other, others)

    def forward(first, last, outs):
        size = (last - first) * tokens
        return kernel_call(
            functools.partial(forward_kernel, last - first, experts, first),
            (scalar, gate_up_w, down_w, *rows_fwd[first:last]),
            outs,
            3 * flops * (last - first) // owners,
            [
                pltpu.VMEM((size, 2 * hidden_width), jnp.float32),
                pltpu.VMEM((size, LANES), jnp.float32),
                pltpu.VMEM((size, hidden_width), jnp.bfloat16),
            ],
            1,
        )

    own, near, back, back_other, others = forward(
        0, early, [block_of(1, width)] * 4 + [block_of(2, width)]
    )
    far, far_other = forward(early, owners, [block_of(1, width)] * 2)

    half = 3 * hidden_width // 2

    def ring_sum(away, start, terms):
        pairs = [(i, (i + away) % replicas) for i in range(replicas)]
        running = start
        for hop in range(1, len(terms) + 2):
            if hop > 1:
                term = terms[hop - 2].astype(jnp.float32)
                added = moved.astype(jnp.float32)
                if hop == 2:
                    kept = (term[half:], term[:half])[away < 0]
                    summed = (term[:half], term[half:])[away < 0] + added
                    running = jnp.concatenate([summed, kept] if away > 0 else [kept, summed], axis=0)
                else:
                    running = term + added
                running = running.astype(jnp.bfloat16)
            moved = lax.ppermute(running, "dp", pairs)
        return moved.astype(jnp.float32)

    farthest = left_parts[lefts - 1]
    weight_sums = ring_sum(1, farthest[:half], [left_parts[i] for i in range(lefts - 2, 0, -1)])
    weight_sums += ring_sum(-1, farthest[half:], [right_parts[i] for i in range(replicas - lefts)])
    weight_sums = (weight_sums + left_parts[0].astype(jnp.float32)).astype(jnp.bfloat16)
    normed_grad = back_rows[:, :width]
    inner_mean = jnp.mean(normed_grad * unit_bwd, axis=1, keepdims=True)
    grad_value = upstream.astype(jnp.float32) + (normed_grad - unit_bwd * inner_mean) * inverse_bwd
    input_grad = grad_value.astype(jnp.bfloat16)
    section_value = scatter_sum((own, near, back, far), far_other, back_other, others, inputs_fwd)
    section_out = section_value.astype(jnp.bfloat16)

    grad_gate_up = weight_sums[: 2 * hidden_width].T
    grad_down = weight_sums[2 * hidden_width :]
    router_sum = back_rows[: replicas * experts, width : width + share // owners]
    router_sum = router_sum.reshape(replicas, experts, share // owners)
    router_sum = lax.all_to_all(router_sum, "dp", split_axis=0, concat_axis=0, tiled=True)
    router_sum = jnp.sum(router_sum, axis=0)
    grad_router = router_sum.T
    return (
        section_out[None],
        input_grad[None],
        grad_gate_up[None, None],
        grad_down[None, None],
        grad_router[None],
    )


def solution(mesh):
    placed = (
        P(("dp", "expert"), None),
        P(("dp", "expert"), None),
        P("pipe", ("dp", "expert"), None),
        P("pipe", ("dp", "expert"), None),
        P("pipe", ("dp", "expert"), None),
        P("pipe", ("dp", "expert"), None),
        P("pipe", ("dp", "expert"), None),
        P("pipe", None, None),
        P("pipe", "expert", None, None),
        P("pipe", "expert", None, None),
    )
    return jax.shard_map(
        section_step,
        mesh=mesh,
        in_specs=placed,
        out_specs=(
            P("pipe", ("dp", "expert"), None),
            P("pipe", ("dp", "expert"), None),
            P("pipe", "expert", "dp", None),
            P("pipe", "expert", None, "dp"),
            P("pipe", ("dp", "expert"), None),
        ),
        check_vma=False,
    )
```

```python
import functools

import jax
import jax.numpy as jnp
from jax import lax
from jax.experimental import pallas as pl
from jax.experimental.pallas import tpu as pltpu
from jax.sharding import PartitionSpec as P


EPSILON = 1e-05
LANES = 128
ROUTER_ROWS = 16
CHUNK = 512


def passed_along(x, axis, by):
    length = lax.axis_size(axis)
    pairs = [(i, i + by) for i in range(length) if 0 <= i + by < length]
    return lax.ppermute(x, axis, pairs)


def ring_pairs(away):
    chips = lax.axis_size("expert") // 2
    pairs = []
    for chip in range(chips):
        for core in range(2):
            step = away if core == 0 else -away
            pairs.append((2 * chip + core, 2 * ((chip + step) % chips) + core))
    return pairs


def ahead(x):
    return lax.ppermute(x, "expert", ring_pairs(1))


def behind(x):
    return lax.ppermute(x, "expert", ring_pairs(-1))


def swapped(x):
    return lax.ppermute(x, "expert", [(i, i ^ 1) for i in range(lax.axis_size("expert"))])


def gather(block):
    near = ahead(block)
    back = behind(block)
    own_other = swapped(block)
    far = ahead(near)
    near_other = swapped(near)
    back_other = swapped(back)
    far_other = swapped(far)
    return [block, own_other, near, near_other, back, back_other, far, far_other]


def scatter_sum(mine, far_other, back_other, others):
    own, near, back, far = mine
    tokens = own.shape[0]

    def wide(x):
        return x.astype(jnp.float32)

    far_other = swapped(far_other)
    back_other = swapped(back_other)
    others = swapped(others)
    far = (wide(far) + wide(far_other)).astype(jnp.bfloat16)
    passing = behind(far)
    back = (wide(back) + wide(back_other)).astype(jnp.bfloat16)
    from_back = ahead(back)
    near = (wide(near) + wide(others[:tokens]) + wide(passing)).astype(jnp.bfloat16)
    from_near = behind(near)
    return wide(own) + wide(others[tokens:]) + wide(from_back) + wide(from_near)


def contract_cols(first_operand, second_operand):
    return lax.dot_general(
        first_operand, second_operand, (((1,), (1,)), ((), ())), preferred_element_type=jnp.float32
    )


def stacked(blocks, columns):
    return jnp.concatenate([block[:, columns] for block in blocks], axis=0)


def over_chunks(width, chunk, step):
    def body(index, carry):
        step(index, pl.ds(pl.multiple_of(index * chunk, chunk), chunk))
        return carry

    lax.fori_loop(0, width // chunk, body, 0)


def over_rows(count, step):
    def body(index, carry):
        step(pl.ds(pl.multiple_of(index * LANES, LANES), LANES))
        return carry

    lax.fori_loop(0, count // LANES, body, 0)


def read_side(columns, experts, mine):
    table = columns[:, :experts] + columns[:, experts : 2 * experts]
    lane = lax.broadcasted_iota(jnp.int32, table.shape, 1)
    weight = jnp.sum(jnp.where(lane == mine, table, 0.0), axis=1, keepdims=True)
    inverse = columns[:, 2 * experts : 2 * experts + 1] + columns[:, 2 * experts + 1 : 2 * experts + 2]
    return (table, lane, weight, inverse)


def project_kernel(owners, *refs):
    blocks, gate_up, projected = refs[:owners], refs[owners], refs[owners + 1]
    projected[...] = jnp.zeros_like(projected)

    def step(index, columns):
        projected[...] += jnp.dot(
            stacked(blocks, columns), gate_up[columns, :], preferred_element_type=jnp.float32
        )

    over_chunks(gate_up.shape[0], CHUNK, step)


def middle_kernel(owners, experts, first_row, *refs):
    mine_ref, projected_ref, down = refs[:3]
    blocks = refs[3 : 3 + owners]
    grads, steps, first_turned, second_turned, bare, side = refs[3 + owners :]
    hidden_width, width = down.shape
    count = grads.shape[0]
    mine = mine_ref[0]
    bare[...] = jnp.zeros_like(bare)
    side[...] = stacked(blocks, slice(width, width + LANES)).astype(jnp.float32)

    def step(index, columns):
        bare[...] += contract_cols(stacked(blocks, columns), down[:, columns])

    over_chunks(width, CHUNK, step)

    def finish(rows):
        table, lane, weight, inverse = read_side(side[rows, :], experts, mine)
        projected = projected_ref[pl.ds(rows.start + first_row, LANES), :] * inverse
        pre_gate = projected[:, :hidden_width]
        pre_up = projected[:, hidden_width:]
        sigmoid_gate = jax.nn.sigmoid(pre_gate)
        active = pre_gate * sigmoid_gate
        hidden = active * pre_up
        bare_grad = bare[rows, :]
        gate_grad = jnp.sum(hidden * bare_grad, axis=1, keepdims=True)
        hidden_grad = bare_grad * weight
        grad_g = hidden_grad * pre_up * sigmoid_gate * (1.0 + pre_gate * (1.0 - sigmoid_gate))
        grad_u = hidden_grad * active
        other = jnp.sum(table, axis=1, keepdims=True) - weight
        sign = jnp.where(lane == mine, 1.0, jnp.where(table > 0.0, -1.0, 0.0))
        logit_part = weight * other * gate_grad * sign
        logit_part = jnp.concatenate(
            [logit_part, jnp.zeros((LANES, LANES - experts), jnp.float32)], axis=1
        )
        grads[rows, :hidden_width] = grad_g.astype(jnp.bfloat16)
        grads[rows, hidden_width:] = grad_u.astype(jnp.bfloat16)
        steps[rows, :] = logit_part.astype(jnp.bfloat16)
        first_turned[:hidden_width, rows] = (grad_g * inverse).T.astype(jnp.bfloat16)
        first_turned[hidden_width : 2 * hidden_width, rows] = (grad_u * inverse).T.astype(jnp.bfloat16)
        first_turned[2 * hidden_width :, rows] = (logit_part * inverse).T[:ROUTER_ROWS].astype(
            jnp.bfloat16
        )
        second_turned[:, rows] = (hidden * weight).T.astype(jnp.bfloat16)

    over_rows(count, finish)


def weights_kernel(owners, *refs):
    replica_ref, turned, refs = refs[0], refs[1:5], refs[5:]
    rows, ups = refs[:owners], refs[owners : 2 * owners]
    left_out, right_out, router_out = refs[2 * owners :]
    _, share = left_out.shape[1:]
    replicas = left_out.shape[0] + right_out.shape[0]
    lefts = left_out.shape[0]
    middle = turned[0].shape[0] - ROUTER_ROWS
    experts = router_out.shape[0] // replicas
    replica = replica_ref[0]

    def chunk(shift, carry):
        target = (replica + shift) % replicas

        columns = pl.ds(pl.multiple_of(target * share, share), share)
        first = jnp.dot(
            jnp.concatenate([turned[0][...], turned[1][...]], axis=1),
            stacked(rows, columns),
            preferred_element_type=jnp.float32,
        )
        second = jnp.dot(
            jnp.concatenate([turned[2][...], turned[3][...]], axis=1),
            stacked(ups, columns),
            preferred_element_type=jnp.float32,
        )

        def put(out, slot):
            out[slot, :middle, :] = first[:middle].astype(jnp.bfloat16)
            out[slot, middle:, :] = second.astype(jnp.bfloat16)

        @pl.when(shift < lefts)
        def _():
            put(left_out, shift)

        @pl.when(shift >= lefts)
        def _():
            put(right_out, shift - lefts)

        line = pl.ds(pl.multiple_of((target ^ replica) * experts, experts), experts)
        router_out[line, :] = first[middle : middle + experts]
        return carry

    lax.fori_loop(0, replicas, chunk, 0)


def store_rows(result, columns, mine, far_other, back_other, others, first, tokens):
    places = [(mine[0], 0), (others, 1), (mine[1], 0), (others, 0), (mine[2], 0), (back_other, 0)]
    places = [*places, (mine[3], 0), (far_other, 0)]
    for index in range(result.shape[0] // tokens):
        out, slot = places[first + index]
        rows = slice(slot * tokens, (slot + 1) * tokens)
        out[rows, columns] = result[index * tokens : (index + 1) * tokens].astype(jnp.bfloat16)


def rows_kernel(owners, *refs):
    mine_ref, early_grads, late_grads, early_steps, late_steps, gate_up, router_turned, router_part = refs[:8]
    own, near, back, far, far_other, back_other, others, side = refs[8:]
    mine_refs = (own, near, back, far)
    tokens = own.shape[0]
    width = gate_up.shape[0]
    lines, share = router_part.shape
    piece = share // owners

    def step(index, columns):
        result = contract_cols(
            jnp.concatenate([early_grads[...], late_grads[...]], axis=0), gate_up[columns, :]
        )
        result += jnp.dot(
            jnp.concatenate([early_steps[...], late_steps[...]], axis=0),
            router_turned[:, columns],
            preferred_element_type=jnp.float32,
        )
        store_rows(result, columns, mine_refs, far_other, back_other, others, 0, tokens)

    over_chunks(width, CHUNK, step)
    me = mine_ref[0]
    chips = owners // 2
    chip, core = me // 2, me % 2
    way = 1 - 2 * core
    part = router_part[...].astype(jnp.bfloat16)
    row = lax.broadcasted_iota(jnp.int32, (share, LANES), 0)
    lane = lax.broadcasted_iota(jnp.int32, (share, LANES), 1)
    side[...] = jnp.zeros_like(side)

    def block(index, carry):
        pair, crossed = index // 2, index % 2
        back_way = way * (1 - 2 * crossed)
        move = jnp.where(pair == 1, -back_way, jnp.where(pair == 2, back_way, jnp.where(pair == 3, 2, 0)))
        owner = 2 * ((chip + move + chips) % chips) + jnp.where(crossed == 1, 1 - core, core)
        hot = jnp.where((row == owner * piece + lane) & (lane < piece), 1.0, 0.0).astype(jnp.bfloat16)
        block_rows = pl.ds(pl.multiple_of(index * tokens, tokens), lines)
        side[block_rows, :] = jnp.dot(part, hot, preferred_element_type=jnp.float32)
        return carry

    lax.fori_loop(0, owners, block, 0)
    store_rows(
        side[...],
        slice(width, width + LANES),
        mine_refs,
        far_other,
        back_other,
        others,
        0,
        tokens,
    )


def forward_kernel(owners, experts, first, *refs):
    mine_ref, gate_up, down = refs[:3]
    blocks, outs = refs[3 : 3 + owners], refs[3 + owners : -3]
    projected_ref, side, hidden_ref = refs[-3:]
    hidden_width, width = down.shape
    tokens = blocks[0].shape[0]
    projected_ref[...] = jnp.zeros_like(projected_ref)

    def project(index, columns):
        projected_ref[...] += jnp.dot(
            stacked(blocks, columns), gate_up[columns, :], preferred_element_type=jnp.float32
        )

    over_chunks(width, CHUNK, project)
    side[...] = stacked(blocks, slice(width, width + LANES)).astype(jnp.float32)

    def finish(rows):
        _, _, weight, inverse = read_side(side[rows, :], experts, mine_ref[0])
        projected = projected_ref[rows, :] * inverse
        pre_gate = projected[:, :hidden_width]
        pre_up = projected[:, hidden_width:]
        hidden_ref[rows, :] = (pre_gate * jax.nn.sigmoid(pre_gate) * pre_up * weight).astype(jnp.bfloat16)

    over_rows(side.shape[0], finish)
    if first:
        mine, far_other, back_other, others = (None, None, None, outs[0]), outs[1], None, None
    else:
        mine, far_other, back_other, others = (*outs[:3], None), None, outs[3], outs[4]

    def step(index, columns):
        result = jnp.dot(hidden_ref[...], down[:, columns], preferred_element_type=jnp.float32)
        store_rows(result, columns, mine, far_other, back_other, others, first, tokens)

    over_chunks(width, CHUNK, step)


def kernel_call(kernel, operands, outs, flops, scratch=(), scalars=0):
    whole = pl.BlockSpec(memory_space=pltpu.VMEM)
    scalar = pl.BlockSpec(memory_space=pltpu.SMEM)
    return pl.pallas_call(
        kernel,
        out_shape=outs,
        in_specs=[scalar] * scalars + [whole] * (len(operands) - scalars),
        out_specs=[whole] * len(outs),
        scratch_shapes=list(scratch),
        compiler_params=pltpu.CompilerParams(vmem_limit_bytes=12 << 20),
        cost_estimate=pl.CostEstimate(flops=flops, bytes_accessed=10_000_000, transcendentals=0),
    )(*operands)


def inverse_spread(values):
    values = values.astype(jnp.float32)
    return lax.rsqrt(jnp.mean(values * values, axis=-1, keepdims=True) + EPSILON)


def gate_pair(normed, router_w, routes):
    experts = router_w.shape[1]
    logits = jnp.dot(normed, router_w, preferred_element_type=jnp.float32)
    onehot = (routes[:, :, None] == jnp.arange(experts, dtype=jnp.int32)[None, None, :]).astype(
        jnp.float32
    )
    chosen = jnp.sum(onehot * logits[:, None, :], axis=2)
    return (
        jax.nn.sigmoid(chosen[:, 0:1] - chosen[:, 1:2]),
        jax.nn.sigmoid(chosen[:, 1:2] - chosen[:, 0:1]),
    )


def side_columns(gates, routes, inverse, experts):
    lane = jnp.arange(LANES, dtype=jnp.int32)[None, :]
    places = (routes[:, 0:1], routes[:, 1:2], jnp.full_like(routes[:, 0:1], 2 * experts))
    low_shift = (experts, experts, 1)
    total = jnp.zeros((routes.shape[0], LANES), jnp.float32)
    for value, place, shift in zip((*gates, inverse), places, low_shift):
        high = lax.reduce_precision(value, exponent_bits=8, mantissa_bits=7)
        total += jnp.where(lane == place, high, 0.0)
        total += jnp.where(lane == place + shift, value - high, 0.0)
    return total.astype(jnp.bfloat16)


def section_step(
    fresh, cotangent, prev_out, prev_grad, saved_in, route_fwd, route_bwd, router, gate_up, down
):
    section_index = lax.axis_index("pipe")
    sections = lax.axis_size("pipe")
    replicas = lax.axis_size("dp")
    owners = lax.axis_size("expert")
    mine = lax.axis_index("expert")
    inputs_bwd = saved_in[0]
    router_w = router[0]
    gate_up_w = gate_up[0, 0]
    down_w = down[0, 0]
    tokens, width = fresh.shape
    experts = router_w.shape[1]
    hidden_width = down_w.shape[0]

    rows_bwd = gather(inputs_bwd)
    returned = passed_along(prev_grad[0], "pipe", -1)
    arrived = passed_along(prev_out[0], "pipe", 1)
    inverse_bwd = inverse_spread(inputs_bwd)
    unit_bwd = inputs_bwd.astype(jnp.float32) * inverse_bwd
    gates = gate_pair(unit_bwd.astype(jnp.bfloat16), router_w, route_bwd[0])
    upstream = jnp.where(section_index == sections - 1, cotangent, returned)
    side = side_columns(gates, route_bwd[0], inverse_bwd, experts)
    ups = gather(jnp.concatenate([upstream, side], axis=1))

    inputs_fwd = jnp.where(section_index == 0, fresh, arrived)
    inverse_fwd = inverse_spread(inputs_fwd)
    normed_fwd = (inputs_fwd.astype(jnp.float32) * inverse_fwd).astype(jnp.bfloat16)
    gates = gate_pair(normed_fwd, router_w, route_fwd[0])
    side = side_columns(gates, route_fwd[0], inverse_fwd, experts)
    rows_fwd = gather(jnp.concatenate([inputs_fwd, side], axis=1))

    count = owners * tokens
    share = width // replicas
    scalar = mine.astype(jnp.int32).reshape(1)
    router_turned = jnp.pad(router_w.T, ((0, LANES - experts), (0, 0)))
    flops = 2 * count * width * hidden_width
    (projected,) = kernel_call(
        functools.partial(project_kernel, owners),
        (*rows_bwd, gate_up_w),
        [jax.ShapeDtypeStruct((count, 2 * hidden_width), jnp.float32)],
        2 * flops,
    )
    early = owners - 2

    def middle(first, last):
        size = (last - first) * tokens
        return kernel_call(
            functools.partial(middle_kernel, last - first, experts, first * tokens),
            (scalar, projected, down_w, *ups[first:last]),
            [
                jax.ShapeDtypeStruct((size, 2 * hidden_width), jnp.bfloat16),
                jax.ShapeDtypeStruct((size, LANES), jnp.bfloat16),
                jax.ShapeDtypeStruct((2 * hidden_width + ROUTER_ROWS, size), jnp.bfloat16),
                jax.ShapeDtypeStruct((hidden_width, size), jnp.bfloat16),
            ],
            flops * (last - first) // owners,
            [pltpu.VMEM((size, hidden_width), jnp.float32), pltpu.VMEM((size, LANES), jnp.float32)],
            1,
        )

    early_grads, early_steps, early_first, early_second = middle(0, early)
    late_grads, late_steps, late_first, late_second = middle(early, owners)
    place = lax.axis_index("dp").astype(jnp.int32).reshape(1)
    lefts = replicas // 2 + 1
    left_parts, right_parts, router_part = kernel_call(
        functools.partial(weights_kernel, owners),
        (place, early_first, late_first, early_second, late_second, *rows_bwd, *ups),
        [
            jax.ShapeDtypeStruct((lefts, 3 * hidden_width, share), jnp.bfloat16),
            jax.ShapeDtypeStruct((replicas - lefts, 3 * hidden_width, share), jnp.bfloat16),
            jax.ShapeDtypeStruct((replicas * experts, share), jnp.float32),
        ],
        3 * flops,
        (),
        1,
    )

    def block_of(number, wide):
        return jax.ShapeDtypeStruct((number * tokens, wide), jnp.bfloat16)

    wide = width + LANES
    own, near, back, far, far_other, back_other, others = kernel_call(
        functools.partial(rows_kernel, owners),
        (
            scalar,
            early_grads,
            late_grads,
            early_steps,
            late_steps,
            gate_up_w,
            router_turned,
            router_part,
        ),
        [block_of(1, wide)] * 6 + [block_of(2, wide)],
        2 * flops,
        [pltpu.VMEM((count, LANES), jnp.float32)],
        1,
    )
    back_rows = scatter_sum((own, near, back, far), far_other, back_other, others)

    def forward(first, last, outs):
        size = (last - first) * tokens
        return kernel_call(
            functools.partial(forward_kernel, last - first, experts, first),
            (scalar, gate_up_w, down_w, *rows_fwd[first:last]),
            outs,
            3 * flops * (last - first) // owners,
            [
                pltpu.VMEM((size, 2 * hidden_width), jnp.float32),
                pltpu.VMEM((size, LANES), jnp.float32),
                pltpu.VMEM((size, hidden_width), jnp.bfloat16),
            ],
            1,
        )

    own, near, back, back_other, others = forward(
        0, early, [block_of(1, width)] * 4 + [block_of(2, width)]
    )
    far, far_other = forward(early, owners, [block_of(1, width)] * 2)

    def ring_sum(away, terms):
        pairs = [(i, (i + away) % replicas) for i in range(replicas)]
        running = terms[0]
        for hop in range(1, len(terms) + 1):
            if hop > 1:
                term = terms[hop - 1]
                running = (moved.astype(jnp.float32) + term.astype(jnp.float32)).astype(jnp.bfloat16)
            moved = lax.ppermute(running, "dp", pairs)
        return moved.astype(jnp.float32)

    weight_sums = ring_sum(1, [left_parts[i] for i in range(lefts - 1, 0, -1)])
    weight_sums += ring_sum(-1, [right_parts[i] for i in range(replicas - lefts)])
    weight_sums = (weight_sums + left_parts[0].astype(jnp.float32)).astype(jnp.bfloat16)
    normed_grad = back_rows[:, :width]
    inner_mean = jnp.mean(normed_grad * unit_bwd, axis=1, keepdims=True)
    grad_value = upstream.astype(jnp.float32) + (normed_grad - unit_bwd * inner_mean) * inverse_bwd
    input_grad = grad_value.astype(jnp.bfloat16)
    back_fwd = scatter_sum((own, near, back, far), far_other, back_other, others)
    section_out = (inputs_fwd.astype(jnp.float32) + back_fwd).astype(jnp.bfloat16)

    grad_gate_up = weight_sums[: 2 * hidden_width].T
    grad_down = weight_sums[2 * hidden_width :]
    router_sum = back_rows[: replicas * experts, width : width + share // owners]
    half = replicas // 2
    while half:
        pairs = [(i, i ^ half) for i in range(replicas)]
        moved = lax.ppermute(router_sum[half * experts :], "dp", pairs)
        router_sum = router_sum[: half * experts] + moved
        half = half // 2
    grad_router = router_sum.T
    return (
        section_out[None],
        input_grad[None],
        grad_gate_up[None, None],
        grad_down[None, None],
        grad_router[None],
    )


def solution(mesh):
    placed = (
        P(("dp", "expert"), None),
        P(("dp", "expert"), None),
        P("pipe", ("dp", "expert"), None),
        P("pipe", ("dp", "expert"), None),
        P("pipe", ("dp", "expert"), None),
        P("pipe", ("dp", "expert"), None),
        P("pipe", ("dp", "expert"), None),
        P("pipe", None, None),
        P("pipe", "expert", None, None),
        P("pipe", "expert", None, None),
    )
    return jax.shard_map(
        section_step,
        mesh=mesh,
        in_specs=placed,
        out_specs=(
            P("pipe", ("dp", "expert"), None),
            P("pipe", ("dp", "expert"), None),
            P("pipe", "expert", "dp", None),
            P("pipe", "expert", None, "dp"),
            P("pipe", ("dp", "expert"), None),
        ),
        check_vma=False,
    )
```

```python
import functools

import jax
import jax.numpy as jnp
from jax import lax
from jax.experimental import pallas as pl
from jax.experimental.pallas import tpu as pltpu
from jax.sharding import PartitionSpec as P


EPSILON = 1e-05
LANES = 128
ROUTER_ROWS = 16
CHUNK = 512


def passed_along(x, axis, by):
    length = lax.axis_size(axis)
    pairs = [(i, i + by) for i in range(length) if 0 <= i + by < length]
    return lax.ppermute(x, axis, pairs)


def ring_pairs(away):
    chips = lax.axis_size("expert") // 2
    pairs = []
    for chip in range(chips):
        for core in range(2):
            step = away if core == 0 else -away
            pairs.append((2 * chip + core, 2 * ((chip + step) % chips) + core))
    return pairs


def ahead(x):
    return lax.ppermute(x, "expert", ring_pairs(1))


def behind(x):
    return lax.ppermute(x, "expert", ring_pairs(-1))


def swapped(x):
    return lax.ppermute(x, "expert", [(i, i ^ 1) for i in range(lax.axis_size("expert"))])


def gather(block):
    near = ahead(block)
    back = behind(block)
    own_other = swapped(block)
    far = ahead(near)
    near_other = swapped(near)
    back_other = swapped(back)
    far_other = swapped(far)
    return [block, own_other, near, near_other, back, back_other, far, far_other]


def scatter_sum(mine, far_other, back_other, others):
    own, near, back, far = mine
    tokens = own.shape[0]

    def wide(x):
        return x.astype(jnp.float32)

    far_other = swapped(far_other)
    if back_other is None:
        far_other, back_other = far_other[:tokens], far_other[tokens:]
    else:
        back_other = swapped(back_other)
    others = swapped(others)
    far = (wide(far) + wide(far_other)).astype(jnp.bfloat16)
    passing = behind(far)
    back = (wide(back) + wide(back_other)).astype(jnp.bfloat16)
    from_back = ahead(back)
    near = (wide(near) + wide(others[:tokens]) + wide(passing)).astype(jnp.bfloat16)
    from_near = behind(near)
    return wide(own) + wide(others[tokens:]) + wide(from_back) + wide(from_near)


def contract_cols(first_operand, second_operand):
    return lax.dot_general(
        first_operand, second_operand, (((1,), (1,)), ((), ())), preferred_element_type=jnp.float32
    )


def stacked(blocks, columns):
    return jnp.concatenate([block[:, columns] for block in blocks], axis=0)


def over_chunks(width, chunk, step):
    def body(index, carry):
        step(index, pl.ds(pl.multiple_of(index * chunk, chunk), chunk))
        return carry

    lax.fori_loop(0, width // chunk, body, 0)


def over_rows(count, step):
    def body(index, carry):
        step(pl.ds(pl.multiple_of(index * LANES, LANES), LANES))
        return carry

    lax.fori_loop(0, count // LANES, body, 0)


def read_side(columns, experts, mine):
    table = columns[:, :experts] + columns[:, experts : 2 * experts]
    lane = lax.broadcasted_iota(jnp.int32, table.shape, 1)
    weight = jnp.sum(jnp.where(lane == mine, table, 0.0), axis=1, keepdims=True)
    inverse = columns[:, 2 * experts : 2 * experts + 1] + columns[:, 2 * experts + 1 : 2 * experts + 2]
    return (table, lane, weight, inverse)


def project_kernel(owners, *refs):
    blocks, gate_up, projected = refs[:owners], refs[owners], refs[owners + 1]
    projected[...] = jnp.zeros_like(projected)

    def step(index, columns):
        projected[...] += jnp.dot(
            stacked(blocks, columns), gate_up[columns, :], preferred_element_type=jnp.float32
        )

    over_chunks(gate_up.shape[0], CHUNK // 2, step)


def middle_kernel(owners, experts, first_row, *refs):
    mine_ref, projected_ref, down = refs[:3]
    blocks = refs[3 : 3 + owners]
    grads, steps, first_turned, second_turned, bare, side = refs[3 + owners :]
    hidden_width, width = down.shape
    count = grads.shape[0]
    mine = mine_ref[0]
    bare[...] = jnp.zeros_like(bare)
    side[...] = stacked(blocks, slice(width, width + LANES)).astype(jnp.float32)

    def step(index, columns):
        bare[...] += contract_cols(stacked(blocks, columns), down[:, columns])

    over_chunks(width, CHUNK, step)

    def finish(rows):
        table, lane, weight, inverse = read_side(side[rows, :], experts, mine)
        projected = projected_ref[pl.ds(rows.start + first_row, LANES), :] * inverse
        pre_gate = projected[:, :hidden_width]
        pre_up = projected[:, hidden_width:]
        sigmoid_gate = jax.nn.sigmoid(pre_gate)
        active = pre_gate * sigmoid_gate
        hidden = active * pre_up
        bare_grad = bare[rows, :]
        gate_grad = jnp.sum(hidden * bare_grad, axis=1, keepdims=True)
        hidden_grad = bare_grad * weight
        grad_g = hidden_grad * pre_up * sigmoid_gate * (1.0 + pre_gate * (1.0 - sigmoid_gate))
        grad_u = hidden_grad * active
        other = jnp.sum(table, axis=1, keepdims=True) - weight
        sign = jnp.where(lane == mine, 1.0, jnp.where(table > 0.0, -1.0, 0.0))
        logit_part = weight * other * gate_grad * sign
        logit_part = jnp.concatenate(
            [logit_part, jnp.zeros((LANES, LANES - experts), jnp.float32)], axis=1
        )
        grads[rows, :hidden_width] = grad_g.astype(jnp.bfloat16)
        grads[rows, hidden_width:] = grad_u.astype(jnp.bfloat16)
        steps[rows, :] = logit_part.astype(jnp.bfloat16)
        first_turned[:hidden_width, rows] = (grad_g * inverse).T.astype(jnp.bfloat16)
        first_turned[hidden_width : 2 * hidden_width, rows] = (grad_u * inverse).T.astype(jnp.bfloat16)
        first_turned[2 * hidden_width :, rows] = (logit_part * inverse).T[:ROUTER_ROWS].astype(
            jnp.bfloat16
        )
        second_turned[:, rows] = (hidden * weight).T.astype(jnp.bfloat16)

    over_rows(count, finish)


def weights_kernel(owners, *refs):
    replica_ref, turned, refs = refs[0], refs[1:5], refs[5:]
    rows, ups = refs[:owners], refs[owners : 2 * owners]
    left_out, right_out, router_out = refs[2 * owners :]
    _, share = left_out.shape[1:]
    replicas = left_out.shape[0] + right_out.shape[0]
    lefts = left_out.shape[0]
    middle = turned[0].shape[0] - ROUTER_ROWS
    experts = router_out.shape[0] // replicas
    replica = replica_ref[0]

    def chunk(shift, carry):
        target = (replica + shift) % replicas

        columns = pl.ds(pl.multiple_of(target * share, share), share)
        first = jnp.dot(
            jnp.concatenate([turned[0][...], turned[1][...]], axis=1),
            stacked(rows, columns),
            preferred_element_type=jnp.float32,
        )
        second = jnp.dot(
            jnp.concatenate([turned[2][...], turned[3][...]], axis=1),
            stacked(ups, columns),
            preferred_element_type=jnp.float32,
        )

        def put(out, slot):
            out[slot, :middle, :] = first[:middle].astype(jnp.bfloat16)
            out[slot, middle:, :] = second.astype(jnp.bfloat16)

        @pl.when(shift < lefts)
        def _():
            put(left_out, shift)

        @pl.when(shift >= lefts)
        def _():
            put(right_out, shift - lefts)

        line = pl.ds(pl.multiple_of((target ^ replica) * experts, experts), experts)
        router_out[line, :] = first[middle : middle + experts]
        return carry

    lax.fori_loop(0, replicas, chunk, 0)


def store_rows(result, columns, mine, far_other, back_other, others, first, tokens):
    back_place = (far_other, 1) if back_other is None else (back_other, 0)
    places = [(mine[0], 0), (others, 1), (mine[1], 0), (others, 0), (mine[2], 0), back_place]
    places = [*places, (mine[3], 0), (far_other, 0)]
    for index in range(result.shape[0] // tokens):
        out, slot = places[first + index]
        rows = slice(slot * tokens, (slot + 1) * tokens)
        out[rows, columns] = result[index * tokens : (index + 1) * tokens].astype(jnp.bfloat16)


def rows_kernel(owners, *refs):
    mine_ref, early_grads, late_grads, early_steps, late_steps, gate_up, router_turned, router_part = refs[:8]
    own, near, back, far, far_other, others, side = refs[8:]
    back_other = None
    mine_refs = (own, near, back, far)
    tokens = own.shape[0]
    width = gate_up.shape[0]
    lines, share = router_part.shape
    piece = share // owners

    def step(index, columns):
        result = contract_cols(
            jnp.concatenate([early_grads[...], late_grads[...]], axis=0), gate_up[columns, :]
        )
        result += jnp.dot(
            jnp.concatenate([early_steps[...], late_steps[...]], axis=0),
            router_turned[:, columns],
            preferred_element_type=jnp.float32,
        )
        store_rows(result, columns, mine_refs, far_other, back_other, others, 0, tokens)

    over_chunks(width, CHUNK, step)
    me = mine_ref[0]
    chips = owners // 2
    chip, core = me // 2, me % 2
    way = 1 - 2 * core
    part = router_part[...].astype(jnp.bfloat16)
    row = lax.broadcasted_iota(jnp.int32, (share, LANES), 0)
    lane = lax.broadcasted_iota(jnp.int32, (share, LANES), 1)
    side[...] = jnp.zeros_like(side)

    def block(index, carry):
        pair, crossed = index // 2, index % 2
        back_way = way * (1 - 2 * crossed)
        move = jnp.where(pair == 1, -back_way, jnp.where(pair == 2, back_way, jnp.where(pair == 3, 2, 0)))
        owner = 2 * ((chip + move + chips) % chips) + jnp.where(crossed == 1, 1 - core, core)
        hot = jnp.where((row == owner * piece + lane) & (lane < piece), 1.0, 0.0).astype(jnp.bfloat16)
        block_rows = pl.ds(pl.multiple_of(index * tokens, tokens), lines)
        side[block_rows, :] = jnp.dot(part, hot, preferred_element_type=jnp.float32)
        return carry

    lax.fori_loop(0, owners, block, 0)
    store_rows(
        side[...],
        slice(width, width + LANES),
        mine_refs,
        far_other,
        back_other,
        others,
        0,
        tokens,
    )


def forward_kernel(owners, experts, first, *refs):
    mine_ref, gate_up, down = refs[:3]
    blocks, outs = refs[3 : 3 + owners], refs[3 + owners : -3]
    projected_ref, side, hidden_ref = refs[-3:]
    hidden_width, width = down.shape
    tokens = blocks[0].shape[0]
    projected_ref[...] = jnp.zeros_like(projected_ref)

    def project(index, columns):
        projected_ref[...] += jnp.dot(
            stacked(blocks, columns), gate_up[columns, :], preferred_element_type=jnp.float32
        )

    over_chunks(width, CHUNK, project)
    side[...] = stacked(blocks, slice(width, width + LANES)).astype(jnp.float32)

    def finish(rows):
        _, _, weight, inverse = read_side(side[rows, :], experts, mine_ref[0])
        projected = projected_ref[rows, :] * inverse
        pre_gate = projected[:, :hidden_width]
        pre_up = projected[:, hidden_width:]
        hidden_ref[rows, :] = (pre_gate * jax.nn.sigmoid(pre_gate) * pre_up * weight).astype(jnp.bfloat16)

    over_rows(side.shape[0], finish)
    if first:
        mine, far_other, back_other, others = (None, None, None, outs[0]), outs[1], None, None
    else:
        mine, far_other, back_other, others = (*outs[:3], None), None, outs[3], outs[4]

    def step(index, columns):
        result = jnp.dot(hidden_ref[...], down[:, columns], preferred_element_type=jnp.float32)
        store_rows(result, columns, mine, far_other, back_other, others, first, tokens)

    over_chunks(width, CHUNK, step)


def kernel_call(kernel, operands, outs, flops, scratch=(), scalars=0):
    whole = pl.BlockSpec(memory_space=pltpu.VMEM)
    scalar = pl.BlockSpec(memory_space=pltpu.SMEM)
    return pl.pallas_call(
        kernel,
        out_shape=outs,
        in_specs=[scalar] * scalars + [whole] * (len(operands) - scalars),
        out_specs=[whole] * len(outs),
        scratch_shapes=list(scratch),
        compiler_params=pltpu.CompilerParams(vmem_limit_bytes=12 << 20),
        cost_estimate=pl.CostEstimate(flops=flops, bytes_accessed=10_000_000, transcendentals=0),
    )(*operands)


def inverse_spread(values):
    values = values.astype(jnp.float32)
    return lax.rsqrt(jnp.mean(values * values, axis=-1, keepdims=True) + EPSILON)


def gate_pair(normed, router_w, routes):
    experts = router_w.shape[1]
    logits = jnp.dot(normed, router_w, preferred_element_type=jnp.float32)
    onehot = (routes[:, :, None] == jnp.arange(experts, dtype=jnp.int32)[None, None, :]).astype(
        jnp.float32
    )
    chosen = jnp.sum(onehot * logits[:, None, :], axis=2)
    return (
        jax.nn.sigmoid(chosen[:, 0:1] - chosen[:, 1:2]),
        jax.nn.sigmoid(chosen[:, 1:2] - chosen[:, 0:1]),
    )


def side_columns(gates, routes, inverse, experts):
    lane = jnp.arange(LANES, dtype=jnp.int32)[None, :]
    places = (routes[:, 0:1], routes[:, 1:2], jnp.full_like(routes[:, 0:1], 2 * experts))
    low_shift = (experts, experts, 1)
    total = jnp.zeros((routes.shape[0], LANES), jnp.float32)
    for value, place, shift in zip((*gates, inverse), places, low_shift):
        high = lax.reduce_precision(value, exponent_bits=8, mantissa_bits=7)
        total += jnp.where(lane == place, high, 0.0)
        total += jnp.where(lane == place + shift, value - high, 0.0)
    return total.astype(jnp.bfloat16)


def section_step(
    fresh, cotangent, prev_out, prev_grad, saved_in, route_fwd, route_bwd, router, gate_up, down
):
    section_index = lax.axis_index("pipe")
    sections = lax.axis_size("pipe")
    replicas = lax.axis_size("dp")
    owners = lax.axis_size("expert")
    mine = lax.axis_index("expert")
    inputs_bwd = saved_in[0]
    router_w = router[0]
    gate_up_w = gate_up[0, 0]
    down_w = down[0, 0]
    tokens, width = fresh.shape
    experts = router_w.shape[1]
    hidden_width = down_w.shape[0]

    rows_bwd = gather(inputs_bwd)
    returned = passed_along(prev_grad[0], "pipe", -1)
    arrived = passed_along(prev_out[0], "pipe", 1)
    inverse_bwd = inverse_spread(inputs_bwd)
    unit_bwd = inputs_bwd.astype(jnp.float32) * inverse_bwd
    gates = gate_pair(unit_bwd.astype(jnp.bfloat16), router_w, route_bwd[0])
    upstream = jnp.where(section_index == sections - 1, cotangent, returned)
    side = side_columns(gates, route_bwd[0], inverse_bwd, experts)
    ups = gather(jnp.concatenate([upstream, side], axis=1))

    inputs_fwd = jnp.where(section_index == 0, fresh, arrived)
    inverse_fwd = inverse_spread(inputs_fwd)
    normed_fwd = (inputs_fwd.astype(jnp.float32) * inverse_fwd).astype(jnp.bfloat16)
    gates = gate_pair(normed_fwd, router_w, route_fwd[0])
    side = side_columns(gates, route_fwd[0], inverse_fwd, experts)
    rows_fwd = gather(jnp.concatenate([inputs_fwd, side], axis=1))

    count = owners * tokens
    share = width // replicas
    scalar = mine.astype(jnp.int32).reshape(1)
    router_turned = jnp.pad(router_w.T, ((0, LANES - experts), (0, 0)))
    flops = 2 * count * width * hidden_width
    (projected,) = kernel_call(
        functools.partial(project_kernel, owners),
        (*rows_bwd, gate_up_w),
        [jax.ShapeDtypeStruct((count, 2 * hidden_width), jnp.float32)],
        2 * flops,
    )
    early = owners - 2

    def middle(first, last):
        size = (last - first) * tokens
        return kernel_call(
            functools.partial(middle_kernel, last - first, experts, first * tokens),
            (scalar, projected, down_w, *ups[first:last]),
            [
                jax.ShapeDtypeStruct((size, 2 * hidden_width), jnp.bfloat16),
                jax.ShapeDtypeStruct((size, LANES), jnp.bfloat16),
                jax.ShapeDtypeStruct((2 * hidden_width + ROUTER_ROWS, size), jnp.bfloat16),
                jax.ShapeDtypeStruct((hidden_width, size), jnp.bfloat16),
            ],
            flops * (last - first) // owners,
            [pltpu.VMEM((size, hidden_width), jnp.float32), pltpu.VMEM((size, LANES), jnp.float32)],
            1,
        )

    early_grads, early_steps, early_first, early_second = middle(0, early)
    late_grads, late_steps, late_first, late_second = middle(early, owners)
    place = lax.axis_index("dp").astype(jnp.int32).reshape(1)
    lefts = replicas // 2 + 1
    left_parts, right_parts, router_part = kernel_call(
        functools.partial(weights_kernel, owners),
        (place, early_first, late_first, early_second, late_second, *rows_bwd, *ups),
        [
            jax.ShapeDtypeStruct((lefts, 3 * hidden_width, share), jnp.bfloat16),
            jax.ShapeDtypeStruct((replicas - lefts, 3 * hidden_width, share), jnp.bfloat16),
            jax.ShapeDtypeStruct((replicas * experts, share), jnp.float32),
        ],
        3 * flops,
        (),
        1,
    )

    def block_of(number, wide):
        return jax.ShapeDtypeStruct((number * tokens, wide), jnp.bfloat16)

    wide = width + LANES
    own, near, back, far, far_other, others = kernel_call(
        functools.partial(rows_kernel, owners),
        (
            scalar,
            early_grads,
            late_grads,
            early_steps,
            late_steps,
            gate_up_w,
            router_turned,
            router_part,
        ),
        [block_of(1, wide)] * 4 + [block_of(2, wide)] * 2,
        2 * flops,
        [pltpu.VMEM((count, LANES), jnp.float32)],
        1,
    )
    back_rows = scatter_sum((own, near, back, far), far_other, None, others)

    def forward(first, last, outs):
        size = (last - first) * tokens
        return kernel_call(
            functools.partial(forward_kernel, last - first, experts, first),
            (scalar, gate_up_w, down_w, *rows_fwd[first:last]),
            outs,
            3 * flops * (last - first) // owners,
            [
                pltpu.VMEM((size, 2 * hidden_width), jnp.float32),
                pltpu.VMEM((size, LANES), jnp.float32),
                pltpu.VMEM((size, hidden_width), jnp.bfloat16),
            ],
            1,
        )

    own, near, back, back_other, others = forward(
        0, early, [block_of(1, width)] * 4 + [block_of(2, width)]
    )
    far, far_other = forward(early, owners, [block_of(1, width)] * 2)

    def ring_sum(away, terms):
        pairs = [(i, (i + away) % replicas) for i in range(replicas)]
        running = terms[0]
        for hop in range(1, len(terms) + 1):
            if hop > 1:
                term = terms[hop - 1]
                running = (moved.astype(jnp.float32) + term.astype(jnp.float32)).astype(jnp.bfloat16)
            moved = lax.ppermute(running, "dp", pairs)
        return moved.astype(jnp.float32)

    weight_sums = ring_sum(1, [left_parts[i] for i in range(lefts - 1, 0, -1)])
    weight_sums += ring_sum(-1, [right_parts[i] for i in range(replicas - lefts)])
    weight_sums = (weight_sums + left_parts[0].astype(jnp.float32)).astype(jnp.bfloat16)
    normed_grad = back_rows[:, :width]
    inner_mean = jnp.mean(normed_grad * unit_bwd, axis=1, keepdims=True)
    grad_value = upstream.astype(jnp.float32) + (normed_grad - unit_bwd * inner_mean) * inverse_bwd
    input_grad = grad_value.astype(jnp.bfloat16)
    back_fwd = scatter_sum((own, near, back, far), far_other, back_other, others)
    section_out = (inputs_fwd.astype(jnp.float32) + back_fwd).astype(jnp.bfloat16)

    grad_gate_up = weight_sums[: 2 * hidden_width].T
    grad_down = weight_sums[2 * hidden_width :]
    router_sum = back_rows[: replicas * experts, width : width + share // owners]
    half = replicas // 2
    while half:
        pairs = [(i, i ^ half) for i in range(replicas)]
        moved = lax.ppermute(router_sum[half * experts :], "dp", pairs)
        router_sum = router_sum[: half * experts] + moved
        half = half // 2
    grad_router = router_sum.T
    return (
        section_out[None],
        input_grad[None],
        grad_gate_up[None, None],
        grad_down[None, None],
        grad_router[None],
    )


def solution(mesh):
    placed = (
        P(("dp", "expert"), None),
        P(("dp", "expert"), None),
        P("pipe", ("dp", "expert"), None),
        P("pipe", ("dp", "expert"), None),
        P("pipe", ("dp", "expert"), None),
        P("pipe", ("dp", "expert"), None),
        P("pipe", ("dp", "expert"), None),
        P("pipe", None, None),
        P("pipe", "expert", None, None),
        P("pipe", "expert", None, None),
    )
    return jax.shard_map(
        section_step,
        mesh=mesh,
        in_specs=placed,
        out_specs=(
            P("pipe", ("dp", "expert"), None),
            P("pipe", ("dp", "expert"), None),
            P("pipe", "expert", "dp", None),
            P("pipe", "expert", None, "dp"),
            P("pipe", ("dp", "expert"), None),
        ),
        check_vma=False,
    )
```
